32 devices in a mesh: gx: 8 (over z, y), gy: 4 (over x, core).
Axes of the slice: x: 2, y: 2, z: 4, core: 2. Of those that a mesh axis runs over, the one named last changes fastest.
Arguments:
- density: float32 [1, 512, 2048], P(None, 'gy', 'gx'), may hold values from 0.5 to 4
- velocity: float32 [2, 1, 512, 2048], P(None, None, 'gy', 'gx'), may hold values from -1 to 1
- energy: float32 [1, 512, 2048], P(None, 'gy', 'gx'), may hold values from 0.5 to 3
- material: int32 [1, 512, 2048], P(None, 'gy', 'gx'), may hold values from 0 to 2
- limiter: int32 [1, 512, 2048], P(None, 'gy', 'gx'), may hold values 0 or 1
- owners: int32 [8192], P(('gx', 'gy')), may hold values from 0 to 7, as said below
- dest_tile: int32 [8192], P(('gx', 'gy')), may hold values from 0 to 255, as said below
- tile_shift: float32 [1, 512], P(None, 'gy'), may hold values from 0.25 to 0.75
Outputs:
- remapped: float32 [4, 1, 512, 2048], P(None, None, 'gy', 'gx')
The draws below stay inside these ranges and needn't reach their ends.
Inputs may be any that keep to these rules, and one draw needn't show every extreme that they name: `owners`: within a plane every mesh row of tiles is rotated along x as a whole by a whole number of tiles, at most 1 either way, and the rotation does not fall from one row to the next; so a tile's owner is its own gx index or the one next to it on either side (wrapping). No device sends more than 128 tiles to either neighbour, and in every draw some device sends exactly 128 to its left neighbour and some exactly 128 to its right one. `dest_tile`: numbered like the owner's own tiles; a destination lies in the tile's own plane and row, and every Eulerian tile is the destination of exactly one Lagrangian tile.
All inputs are finite; a program needn't handle non-finite values. No bound on the sum of `limiter` on one device may be relied on, other than what follows from the above.
Results may differ from the reference program's by a relative error of at most 0.0003.
Values sent between devices are 32-bit elements; how exact they have to be, the bound alone decides.
No kernel may reach another device: no remote copies, remote signals or barrier semaphores. Data moves between devices by JAX's collectives and lax.ppermute only.
A program may use at most 64 MiB of HBM per device.

```python
import math
import jax
import jax.numpy as jnp

PLANES = 1
CY = 128
CX = 256
TILE = 128
NX = 2048
NY = 512
TLAG = 256
TILES = 8192
N_GX = 8
N_GY = 4


def drift_rows(key):
    half_span = CX // TILE // 2
    middle_rows = NY - 2 * CY
    odds = max(2, middle_rows // (2 * half_span + 1))
    plane_keys = jax.random.split(jax.random.fold_in(key, 7321), PLANES)
    row_index = jnp.arange(NY).astype(jnp.int32)

    def one_plane(plane_key):
        draws = jax.random.randint(plane_key, (NY,), 0, odds)
        rising = jnp.where(draws == 0, 1, 0).astype(jnp.int32)
        rising = jnp.where((row_index >= CY) & (row_index < NY - CY), rising, 0)
        level = jnp.clip(jnp.cumsum(rising) - half_span, -half_span, half_span)
        return jnp.where(row_index >= NY - CY, half_span, level)
    return jax.vmap(one_plane)(plane_keys).astype(jnp.int32)


def tile_routes(key):
    rotation = drift_rows(key)
    segments = CX // TILE
    tile_cols = NX // TILE
    columns = jnp.arange(tile_cols).astype(jnp.int32)
    landing = (columns[None, None, :] + rotation[:, :, None]) % tile_cols
    owner_col = landing // segments
    plane_index = jnp.arange(PLANES).astype(jnp.int32)[:, None, None]
    row_index = (jnp.arange(NY).astype(jnp.int32) % CY)[None, :, None]
    local_tile = (plane_index * CY + row_index) * segments + landing % segments
    owner_col = owner_col.reshape(PLANES, N_GY, CY, N_GX, segments).transpose(3, 1, 0, 2, 4).reshape(TILES)
    local_tile = local_tile.reshape(PLANES, N_GY, CY, N_GX, segments).transpose(3, 1, 0, 2, 4).reshape(TILES)
    return (owner_col.astype(jnp.int32), local_tile.astype(jnp.int32))


def draw_owners(key, part):
    return tile_routes(key)[0]


def draw_dest_tile(key, part):
    return tile_routes(key)[1]


def set_ends(values, key, low, top_value):
    longest = values.shape.index(max(values.shape))
    spots = []
    for shift in (0, 1):
        where = [jax.random.randint(jax.random.fold_in(key, axis), (), 0, length) for axis, length in enumerate(values.shape)]
        where[longest] = (where[longest] + shift) % values.shape[longest]
        spots.append(tuple(where))
    return values.at[spots[0]].set(low).at[spots[1]].set(top_value)


def level_of(stream_key, shape, cuts, low, high):
    def one(position, shards_of):
        steps = jax.random.uniform(jax.random.fold_in(jax.random.fold_in(stream_key, 6), position), (shards_of,), jnp.float32, low / len(cuts), high / len(cuts))
        return jnp.repeat(jnp.exp(steps), shape[position] // shards_of).reshape((-1,) + (1,) * (len(shape) - position - 1))

    loudness = one(*cuts[0])
    for cut in cuts[1:]:
        loudness = loudness * one(*cut)
    return loudness


def setup_inputs(seed: int = 0) -> dict:
    key_list = jax.random.split(jax.random.key(seed), 9)
    density = jnp.clip(jnp.exp(math.log(4.0) - 2.0794415 * jax.random.uniform(key_list[0], (PLANES, NY, NX), jnp.float32) ** level_of(key_list[0], (PLANES, NY, NX), ((1, 4), (2, 8)), -0.2, 0.2)), 0.5, 4.0)
    velocity = jnp.clip(jax.random.uniform(key_list[1], (2, PLANES, NY, NX), jnp.float32, -1.0, 1.0) * level_of(key_list[1], (2, PLANES, NY, NX), ((2, 4), (3, 8)), -0.4, 0.0), -1.0, 1.0)
    energy = jnp.clip(0.5 + 2.5 * jax.random.uniform(key_list[2], (PLANES, NY, NX), jnp.float32) ** level_of(key_list[2], (PLANES, NY, NX), ((1, 4), (2, 8)), -0.2, 0.2), 0.5, 3.0)
    material = set_ends(jax.random.randint(key_list[3], (PLANES, NY, NX), 0, 3), jax.random.fold_in(key_list[3], 1), 0, 2).astype(jnp.int32)
    limiter = set_ends((jax.random.randint(key_list[4], (PLANES, NY, NX), 0, 2) < 1).astype(jnp.int32), jax.random.fold_in(key_list[4], 1), 0, 1)
    owners = draw_owners(jax.random.fold_in(key_list[8], 71), 0)
    dest_tile = draw_dest_tile(jax.random.fold_in(key_list[8], 71), 0)
    tile_shift = jnp.clip(0.25 + 0.5 * jax.random.uniform(key_list[7], (PLANES, NY), jnp.float32) ** level_of(key_list[7], (PLANES, NY), ((1, 4),), -0.2, 0.2), 0.25, 0.75)
    return dict(density=density, velocity=velocity, energy=energy, material=material, limiter=limiter, owners=owners, dest_tile=dest_tile, tile_shift=tile_shift)


time_step = 0.05

def heat_ratio(material):
    return jnp.where(material == 0, 1.4, jnp.where(material == 1, 5.0 / 3.0, 3.0)).astype(jnp.float32)

def corners(grid_field):
    return (grid_field[..., :-1, :-1], grid_field[..., :-1, 1:], grid_field[..., 1:, :-1], grid_field[..., 1:, 1:])

def node_velocity(impedance, pressure, speed_x, speed_y):
    weights = corners(impedance)
    pushes = corners(pressure)
    along_x = corners(speed_x)
    along_y = corners(speed_y)
    totals = weights[0] + weights[1] + weights[2] + weights[3]
    moment_x = weights[0] * along_x[0] + weights[1] * along_x[1] + weights[2] * along_x[2] + weights[3] * along_x[3]
    moment_y = weights[0] * along_y[0] + weights[1] * along_y[1] + weights[2] * along_y[2] + weights[3] * along_y[3]
    node_x = (moment_x + (pushes[0] - pushes[1] + pushes[2] - pushes[3])) / totals
    node_y = (moment_y + (pushes[0] + pushes[1] - pushes[2] - pushes[3])) / totals
    return (node_x, node_y)

def cell_update(impedance, pressure, speed_x, speed_y, density, energy_total, node_x, node_y):
    nodes_x = corners(node_x)
    nodes_y = corners(node_y)
    sum_x = nodes_x[0] + nodes_x[1] + nodes_x[2] + nodes_x[3]
    sum_y = nodes_y[0] + nodes_y[1] + nodes_y[2] + nodes_y[3]
    force_x = 0.5 * impedance * (sum_x - 4.0 * speed_x)
    force_y = 0.5 * impedance * (sum_y - 4.0 * speed_y)
    volume_rate = 0.5 * (-nodes_x[0] - nodes_y[0] + nodes_x[1] - nodes_y[1] - nodes_x[2] + nodes_y[2] + nodes_x[3] + nodes_y[3])
    relaxation = jnp.zeros_like(speed_x)
    for corner in range(4):
        relaxation = relaxation + (nodes_x[corner] - speed_x) * nodes_x[corner] + (nodes_y[corner] - speed_y) * nodes_y[corner]
    work_rate = -pressure * volume_rate + 0.5 * impedance * relaxation
    conserved = jnp.stack([density, density * speed_x + time_step * force_x, density * speed_y + time_step * force_y, energy_total + time_step * work_rate])
    left_speed = 0.5 * (nodes_x[0] + nodes_x[2])
    right_speed = 0.5 * (nodes_x[1] + nodes_x[3])
    widths = 1.0 + time_step * (right_speed - left_speed)
    return (conserved / widths, left_speed, right_speed)

def minmod(left_side, right_side):
    return jnp.where(left_side * right_side > 0, jnp.sign(left_side) * jnp.minimum(jnp.abs(left_side), jnp.abs(right_side)), 0.0)

def centred(left_side, right_side):
    limit_mag = jnp.minimum(jnp.minimum(2.0 * jnp.abs(left_side), 2.0 * jnp.abs(right_side)), 0.5 * jnp.abs(left_side + right_side))
    return jnp.where(left_side * right_side > 0, jnp.sign(left_side) * limit_mag, 0.0)

def limited(values, neighbour_left, neighbour_right, limiter):
    widened = jnp.concatenate([neighbour_left, values, neighbour_right], axis=-1)
    back_diff = values - widened[..., :-2]
    fore_diff = widened[..., 2:] - values
    return jnp.where(limiter == 1, centred(back_diff, fore_diff), minmod(back_diff, fore_diff))

def integrate(values, slopes, left_pos, right_pos):
    cell_pos = jnp.arange(values.shape[-1]).astype(jnp.float32)
    centre = 0.5 * (left_pos + right_pos)
    low_own = jnp.maximum(left_pos, cell_pos)
    high_own = jnp.minimum(right_pos, cell_pos + 1.0)
    span_own = jnp.maximum(high_own - low_own, 0.0)
    offset_own = 0.5 * (high_own + low_own) - centre
    low_next = jnp.maximum(left_pos, cell_pos + 1.0)
    high_next = jnp.minimum(right_pos, cell_pos + 2.0)
    span_next = jnp.maximum(high_next - low_next, 0.0)
    offset_next = 0.5 * (high_next + low_next) - centre
    part_own = span_own[..., None, :] * (values + slopes * offset_own[..., None, :])
    part_next = span_next[..., None, :] * (values + slopes * offset_next[..., None, :])
    empty_col = jnp.zeros_like(part_next[..., :1])
    main_part = part_own + jnp.concatenate([empty_col, part_next[..., :-1]], axis=-1)
    return (main_part, part_next[..., -1])

def reference(density, velocity, energy, material, limiter, owners, dest_tile, tile_shift):
    segments = CX // TILE
    ratios = heat_ratio(material)
    pressure = (ratios - 1.0) * density * energy
    impedance = density * jnp.sqrt(ratios * (ratios - 1.0) * energy)
    speed_x = velocity[0]
    speed_y = velocity[1]
    energy_total = density * (energy + 0.5 * (speed_x * speed_x + speed_y * speed_y))
    stacked = jnp.stack([impedance, pressure, speed_x, speed_y])
    padded = jnp.pad(stacked, ((0, 0), (0, 0), (1, 1), (0, 0)))
    padded = jnp.concatenate([padded[..., -1:], padded, padded[..., :1]], axis=-1)
    node_x, node_y = node_velocity(padded[0], padded[1], padded[2], padded[3])
    values, left_speed, right_speed = cell_update(impedance, pressure, speed_x, speed_y, density, energy_total, node_x, node_y)
    slopes = limited(values, values[..., -1:], values[..., :1], limiter)

    def field_tiles(source_field):
        return source_field.reshape(4, PLANES, N_GY, CY, N_GX, segments, TILE).transpose(4, 2, 1, 3, 5, 0, 6).reshape(TILES, 4, TILE)

    def plain_tiles(source_field):
        return source_field.reshape(PLANES, N_GY, CY, N_GX, segments, TILE).transpose(3, 1, 0, 2, 4, 5).reshape(TILES, TILE)
    cell_pos = jnp.arange(TILE).astype(jnp.float32)
    offsets = plain_tiles(jnp.broadcast_to(tile_shift[:, :, None], (PLANES, NY, NX)))[:, :1]
    left_pos = cell_pos + offsets + time_step * plain_tiles(left_speed)
    right_pos = cell_pos + 1.0 + offsets + time_step * plain_tiles(right_speed)
    main_part, spill_part = integrate(field_tiles(values), field_tiles(slopes), left_pos, right_pos)
    tile_ids = jnp.arange(TILES).astype(jnp.int32)
    band_index = tile_ids // TLAG % N_GY
    targets = ((owners * N_GY + band_index) * TLAG + dest_tile).astype(jnp.int32)
    at_end = dest_tile % segments == segments - 1
    next_owner = (owners + 1) % N_GX
    spill_targets = jnp.where(at_end, (next_owner * N_GY + band_index) * TLAG + dest_tile - (segments - 1), targets + 1).astype(jnp.int32)
    gathered = jax.ops.segment_sum(main_part, targets, num_segments=TILES)
    spilled = jax.ops.segment_sum(spill_part, spill_targets, num_segments=TILES)
    gathered = gathered.at[:, :, 0].add(spilled)
    return gathered.reshape(N_GX, N_GY, PLANES, CY, segments, 4, TILE).transpose(5, 2, 1, 3, 0, 4, 6).reshape(4, PLANES, NY, NX)
```

```python
import functools

import jax
import jax.numpy as jnp
from jax import lax
from jax.experimental import pallas as pl
from jax.experimental.pallas import tpu as pltpu
from jax.sharding import PartitionSpec as P

TILE = 128
time_step = 0.05
EDGE = 8
RAW = 6


def near_pairs(count):
    return [(i, i ^ 1) for i in range(count)]


def far_pairs(count, wraps):
    pairs = []
    for i in range(1, count, 2):
        j = i + 1
        if j < count or wraps:
            pairs += [(i, j % count), (j % count, i)]
    return pairs


def acoustic(density, energy, material):
    first, second = material == 0, material == 1
    less_one = jnp.where(first, 0.4, jnp.where(second, 2.0 / 3.0, 2.0)).astype(jnp.float32)
    both = jnp.where(first, 1.4 * 0.4, jnp.where(second, 10.0 / 9.0, 6.0)).astype(jnp.float32)
    return density * jnp.sqrt(both * energy), less_one * density * energy


def column_sums(impedance, pressure, speed_x, speed_y, from_left):
    along_x, along_y = impedance * speed_x, impedance * speed_y
    up, down = along_y + pressure, along_y - pressure
    return (
        from_left(impedance) + impedance,
        from_left(along_x + pressure) + (along_x - pressure),
        from_left(up) + up,
        from_left(down) + down,
    )


def nodes(below, above):
    scale = 1.0 / (below[0] + above[0])
    return (below[1] + above[1]) * scale, (below[2] + above[3]) * scale


def cell_values(impedance, pressure, speed_x, speed_y, density, energy, lower, upper, from_right):
    side_x = lower[0] + upper[0]
    side_y = lower[1] + upper[1]
    rise_y = upper[1] - lower[1]
    square = lower[0] * lower[0] + upper[0] * upper[0] + lower[1] * lower[1] + upper[1] * upper[1]
    far_x = from_right(side_x)
    sum_x = side_x + far_x
    sum_y = side_y + from_right(side_y)
    half_z = (0.5 * time_step) * impedance
    volume = (far_x - side_x) + (rise_y + from_right(rise_y))
    relaxation = (square + from_right(square)) - speed_x * sum_x - speed_y * sum_y
    left = (0.5 * time_step) * side_x
    right = (0.5 * time_step) * far_x
    scale = 1.0 / (1.0 + (right - left))
    total = density * (energy + 0.5 * (speed_x * speed_x + speed_y * speed_y))
    values = (
        density * scale,
        (density * speed_x + half_z * (sum_x - 4.0 * speed_x)) * scale,
        (density * speed_y + half_z * (sum_y - 4.0 * speed_y)) * scale,
        (total + (half_z * relaxation - (0.5 * time_step) * pressure * volume)) * scale,
    )
    return values, left, right


def remap_weights(shift, left, right):
    start = shift + left
    stop = 1.0 + shift + right
    centre = 0.5 * (start + stop)
    low_own, high_own = jnp.maximum(start, 0.0), jnp.minimum(stop, 1.0)
    span_own = jnp.maximum(high_own - low_own, 0.0)
    low_next, high_next = jnp.maximum(start, 1.0), jnp.minimum(stop, 2.0)
    span_next = jnp.maximum(high_next - low_next, 0.0)
    return (
        span_own,
        span_own * (0.5 * (high_own + low_own) - centre),
        span_next,
        span_next * (0.5 * (high_next + low_next) - centre),
    )


def remapped_field(value, steepness, weights, from_left, from_right):
    back = value - from_left(value)
    fore = from_right(back)
    mean = 0.5 * (back + fore)
    rising = jnp.maximum(jnp.minimum(steepness * jnp.minimum(back, fore), mean), 0.0)
    falling = jnp.minimum(jnp.maximum(steepness * jnp.maximum(back, fore), mean), 0.0)
    slope = rising + falling
    own = weights[0] * value + weights[1] * slope
    return own + from_left(weights[2] * value + weights[3] * slope)


class Wide:
    def __init__(self, parts):
        self.parts = tuple(parts)

    def _with(self, other, op):
        if isinstance(other, Wide):
            return Wide(op(a, b) for a, b in zip(self.parts, other.parts))
        return Wide(op(a, other) for a in self.parts)

    def __add__(self, o):
        return self._with(o, lambda a, b: a + b)

    def __radd__(self, o):
        return self._with(o, lambda a, b: b + a)

    def __sub__(self, o):
        return self._with(o, lambda a, b: a - b)

    def __mul__(self, o):
        return self._with(o, lambda a, b: a * b)

    def __rmul__(self, o):
        return self._with(o, lambda a, b: b * a)


def wide_left(lane, parts):
    turned = [pltpu.roll(a, 1, 1) for a in parts]
    return [turned[0]] + [
        jnp.where(lane == 0, turned[i - 1], turned[i]) for i in range(1, len(turned))
    ]


def wide_right(lane, parts):
    width = parts[0].shape[-1]
    turned = [pltpu.roll(a, width - 1, 1) for a in parts]
    return [
        jnp.where(lane == width - 1, turned[i + 1], turned[i]) for i in range(len(turned) - 1)
    ] + [turned[-1]]


def halo_kernel(rho_lo, vel_lo, en_lo, mat_lo, rho_hi, vel_hi, en_hi, mat_hi, near_ref, far_ref):
    even = lax.axis_index("gy") % 2 == 0
    rows = rho_lo.shape[1]

    def stack(rho, vel, en, mat, row):
        pick = slice(row, row + 1)
        z, p = acoustic(rho[0, pick, :], en[0, pick, :], mat[0, pick, :])
        return [z, p, vel[0, 0, pick, :], vel[1, 0, pick, :]]

    bottom = stack(rho_lo, vel_lo, en_lo, mat_lo, 0)
    top = stack(rho_hi, vel_hi, en_hi, mat_hi, rows - 1)
    for k in range(4):
        near_ref[k : k + 1, :] = jnp.where(even, top[k], bottom[k])
        far_ref[k : k + 1, :] = jnp.where(even, bottom[k], top[k])


def block_kernel(
    rho_ref, vel_ref, en_ref, mat_ref, lim_ref, shift_ref, near_ref, far_ref,
    out_ref, first_ref, second_ref, edge_ref,
    sums_ref, node_ref, press_ref, shifts_ref, edges_ref, *, step,
):
    rows, cols = rho_ref.shape[1:]
    halves = range(cols // TILE)
    even_x = lax.axis_index("gx") % 2 == 0
    even_y = lax.axis_index("gy") % 2 == 0
    pad = 8

    def cut(array, h):
        return array[:, h * TILE : (h + 1) * TILE]

    near, far = near_ref[0:4, :], far_ref[0:4, :]
    below = jnp.where(even_y, far, near)
    above = jnp.where(even_y, near, far)
    lane1 = lax.broadcasted_iota(jnp.int32, (1, TILE), 1)
    for halo, at in ((below, pad - 1), (above, pad + rows)):
        parts = [[cut(halo[k : k + 1, :], h) for h in halves] for k in range(4)]
        left1 = lambda a: Wide(wide_left(lane1, a.parts))
        for s, total in enumerate(column_sums(*[Wide(q) for q in parts], left1)):
            for h in halves:
                sums_ref[s, h, at : at + 1, :] = total.parts[h]
    halo = jnp.concatenate([below, above], axis=0)
    lane8 = lax.broadcasted_iota(jnp.int32, (8, TILE), 1)
    corner = pltpu.roll(jnp.where(lane8 < TILE // 2, cut(halo, 0), cut(halo, len(halves) - 1)), EDGE, 1)
    corner = jnp.concatenate([corner, jnp.zeros((TILE - 8, TILE), jnp.float32)], axis=0)
    corner_t = corner.T[0 : 2 * EDGE, :]
    shifts_ref[...] = jnp.broadcast_to(shift_ref[...], (TILE, TILE)).T

    lane = lax.broadcasted_iota(jnp.int32, (step, TILE), 1)
    left = lambda a: Wide(wide_left(lane, a.parts))
    right = lambda a: Wide(wide_right(lane, a.parts))

    def at_rows(i, offset=0):
        return pl.ds(pl.multiple_of(i * step, step) + offset, step)

    def columns(h):
        return slice(h * TILE, (h + 1) * TILE)

    def first_pass(i, _):
        here = at_rows(i)
        rho = [rho_ref[0, here, columns(h)] for h in halves]
        en = [en_ref[0, here, columns(h)] for h in halves]
        mat = [mat_ref[0, here, columns(h)] for h in halves]
        sx = [vel_ref[0, 0, here, columns(h)] for h in halves]
        sy = [vel_ref[1, 0, here, columns(h)] for h in halves]
        both = [acoustic(rho[h], en[h], mat[h]) for h in halves]
        z, p = [b[0] for b in both], [b[1] for b in both]
        for h in halves:
            press_ref[0, h, here, :] = z[h]
            press_ref[1, h, here, :] = p[h]
        totals = column_sums(Wide(z), Wide(p), Wide(sx), Wide(sy), left)
        for s, total in enumerate(totals):
            for h in halves:
                sums_ref[s, h, at_rows(i, pad), :] = total.parts[h]
        lim = [lim_ref[0, here, columns(h)].astype(jnp.float32) for h in (0, len(halves) - 1)]
        mats = [mat[0].astype(jnp.float32), mat[-1].astype(jnp.float32)]
        edge = jnp.zeros((step, TILE), jnp.float32)
        ends = ((rho[0], rho[-1]), (sx[0], sx[-1]), (sy[0], sy[-1]), (en[0], en[-1]), mats, lim)
        for k, (start, stop) in enumerate(ends):
            turned = pltpu.roll(jnp.where(lane < TILE // 2, start, stop), (2 * k + 1) * EDGE, 1)
            edge = jnp.where(lane >= 2 * k * EDGE, turned, edge)
        edges_ref[here, :] = edge
        return 0

    lax.fori_loop(0, rows // step, first_pass, 0)

    def second_pass(i, _):
        for h in halves:
            under = [sums_ref[s, h, at_rows(i, pad - 1), :] for s in range(3)]
            over = [sums_ref[s, h, at_rows(i, pad), :] for s in (0, 1, 3)]
            nx, ny = nodes(under, [over[0], over[1], None, over[2]])
            node_ref[0, h, at_rows(i), :] = nx
            node_ref[1, h, at_rows(i), :] = ny
        return 0

    lax.fori_loop(0, rows // step, second_pass, 0)
    for h in halves:
        under = [sums_ref[s, h, rows + pad - 1 : rows + pad, :] for s in range(3)]
        over = [sums_ref[s, h, rows + pad : rows + pad + 1, :] for s in (0, 1, 3)]
        nx, ny = nodes(under, [over[0], over[1], None, over[2]])
        node_ref[0, h, rows : rows + 1, :] = nx
        node_ref[1, h, rows : rows + 1, :] = ny

    edge_t = edges_ref[...].T
    edge_ref[0 : 2 * RAW * EDGE, :] = edge_t[0 : 2 * RAW * EDGE, :]
    edge_ref[2 * RAW * EDGE :, :] = corner_t
    base = 4 * rows
    for k in range(RAW + 1):
        source = edge_t if k < RAW else corner_t
        at = 2 * k * EDGE if k < RAW else 0
        right_edge, left_edge = source[at : at + EDGE, :], source[at + EDGE : at + 2 * EDGE, :]
        spot = slice(base + k * EDGE, base + (k + 1) * EDGE)
        first_ref[spot, :] = jnp.where(even_x, right_edge, left_edge)
        second_ref[spot, :] = jnp.where(even_x, left_edge, right_edge)

    def third_pass(i, _):
        here = at_rows(i)
        wide = lambda ref, *at: Wide(ref[(*at, here, columns(h))] for h in halves)
        rho, en = wide(rho_ref, 0), wide(en_ref, 0)
        sx, sy = wide(vel_ref, 0, 0), wide(vel_ref, 1, 0)
        z = Wide(press_ref[0, h, here, :] for h in halves)
        p = Wide(press_ref[1, h, here, :] for h in halves)
        lower = [Wide(node_ref[d, h, here, :] for h in halves) for d in range(2)]
        upper = [Wide(node_ref[d, h, at_rows(i, 1), :] for h in halves) for d in range(2)]
        steepness = Wide(lim_ref[0, here, columns(h)].astype(jnp.float32) + 1.0 for h in halves)
        shift = shifts_ref[here, :]
        values, dl, dr = wide_cells(z, p, sx, sy, rho, en, lower, upper, right)
        weights = [remap_weights(shift, dl.parts[h], dr.parts[h]) for h in halves]
        weights = [Wide(w) for w in zip(*weights)]
        for f, value in enumerate(values):
            done = wide_field(value, steepness, weights, left, right)
            for h in halves:
                out_ref[f, here, columns(h)] = done.parts[h]
            ends = done.parts[0], done.parts[-1]
            spot = pl.ds(pl.multiple_of(f * rows + i * step, step), step)
            first_ref[spot, :] = jnp.where(even_x, ends[1], ends[0])
            second_ref[spot, :] = jnp.where(even_x, ends[0], ends[1])
        return 0

    lax.fori_loop(0, rows // step, third_pass, 0)


def wide_cells(z, p, sx, sy, rho, en, lower, upper, from_right):
    halves = range(len(z.parts))
    pieces = []
    for h in halves:
        lx, ly, ux, uy = (q.parts[h] for q in (*lower, *upper))
        pieces.append((lx + ux, ly + uy, uy - ly, lx * lx + ux * ux + ly * ly + uy * uy))
    far = [from_right(Wide(q)).parts for q in zip(*pieces)]
    results = []
    for h in halves:
        queue = [far[k][h] for k in (0, 1, 2, 3)]
        order = iter(queue)
        results.append(
            cell_values(
                z.parts[h], p.parts[h], sx.parts[h], sy.parts[h], rho.parts[h], en.parts[h],
                [q.parts[h] for q in lower], [q.parts[h] for q in upper], lambda _: next(order),
            )
        )
    values = [Wide(results[h][0][f] for h in halves) for f in range(4)]
    return values, Wide(r[1] for r in results), Wide(r[2] for r in results)


def wide_field(value, steepness, weights, left, right):
    back = value - left(value)
    fore = right(back)
    owns, nexts = [], []
    for h in range(len(value.parts)):
        b, f, k = back.parts[h], fore.parts[h], steepness.parts[h]
        mean = 0.5 * (b + f)
        rising = jnp.maximum(jnp.minimum(k * jnp.minimum(b, f), mean), 0.0)
        falling = jnp.minimum(jnp.maximum(k * jnp.maximum(b, f), mean), 0.0)
        slope = rising + falling
        w = [q.parts[h] for q in weights]
        owns.append(w[0] * value.parts[h] + w[1] * slope)
        nexts.append(w[2] * value.parts[h] + w[3] * slope)
    return Wide(owns) + left(Wide(nexts))


def merge_kernel(
    field_ref, edge_ref, first_ref, second_ref, shift_ref, owner_ref, out_ref, patch_ref, *, step
):
    rows, cols = field_ref.shape[1:]
    column, count = lax.axis_index("gx"), lax.axis_size("gx")
    even_x = column % 2 == 0
    base = 4 * rows
    span = 4 * EDGE

    def window(k):
        spot = slice(base + k * EDGE, base + (k + 1) * EDGE)
        from_near, from_far = first_ref[spot, :], second_ref[spot, :]
        return jnp.concatenate(
            [
                jnp.where(even_x, from_far, from_near),
                edge_ref[(2 * k + 1) * EDGE : (2 * k + 2) * EDGE, :],
                edge_ref[2 * k * EDGE : (2 * k + 1) * EDGE, :],
                jnp.where(even_x, from_near, from_far),
            ],
            axis=0,
        )

    left = lambda a: pltpu.roll(a, 1, 0)
    right = lambda a: pltpu.roll(a, span - 1, 0)
    rho, sx, sy, en, mat, lim = (window(k) for k in range(RAW))
    halo = window(RAW)
    z, p = acoustic(rho, en, mat)
    own = column_sums(z, p, sx, sy, left)
    spread = lambda k: jnp.broadcast_to(halo[:, k : k + 1], (span, rows))
    below = column_sums(*(spread(k) for k in range(4)), left)
    above = column_sums(*(spread(k) for k in range(4, 8)), left)
    lane = lax.broadcasted_iota(jnp.int32, (span, rows), 1)
    under = [jnp.where(lane == 0, b, pltpu.roll(a, 1, 1)) for a, b in zip(own, below)]
    over = [jnp.where(lane == rows - 1, b, pltpu.roll(a, rows - 1, 1)) for a, b in zip(own, above)]
    values, dl, dr = cell_values(
        z, p, sx, sy, rho, en, nodes(under, own), nodes(own, over), right
    )
    weights = remap_weights(shift_ref[...], dl, dr)
    fields = [remapped_field(v, lim + 1.0, weights, left, right) for v in values]
    patch_ref[...] = jnp.concatenate(fields, axis=0).T

    owner = owner_ref[...]
    def total(which):
        hits = jnp.where(owner == which, 1.0, 0.0)
        return jnp.sum(jnp.sum(hits, axis=1, keepdims=True), axis=0, keepdims=True)

    to_left = total((column + count - 1) % count)
    to_right = total((column + 1) % count)
    lane = lax.broadcasted_iota(jnp.int32, (step, TILE), 1)
    row_in = lax.broadcasted_iota(jnp.int32, (step, TILE), 0)
    head, tail = lane < 3, lane >= TILE - 2

    def one(i, _):
        here = pl.ds(pl.multiple_of(i * step, step), step)
        row = (row_in + i * step).astype(jnp.float32)
        goes_left, goes_right = row < to_left, row >= rows - to_right
        patch = patch_ref[here, :]
        for f in range(4):
            at_left = pltpu.roll(patch, (-(span * f + EDGE)) % TILE, 1)
            at_right = pltpu.roll(patch, (-(span * f + 3 * EDGE)) % TILE, 1)
            spot = pl.ds(pl.multiple_of(f * rows + i * step, step), step)
            from_near, from_far = first_ref[spot, :], second_ref[spot, :]
            own_0 = jnp.where(head, at_left, field_ref[f, here, 0:TILE])
            own_1 = jnp.where(tail, at_right, field_ref[f, here, TILE:])
            left_tile = jnp.where(tail, at_left, jnp.where(even_x, from_far, from_near))
            right_tile = jnp.where(head, at_right, jnp.where(even_x, from_near, from_far))
            out_ref[f, 0, here, 0:TILE] = jnp.where(
                goes_right, left_tile, jnp.where(goes_left, own_1, own_0)
            )
            out_ref[f, 0, here, TILE:] = jnp.where(
                goes_right, own_0, jnp.where(goes_left, right_tile, own_1)
            )
        return 0

    lax.fori_loop(0, rows // step, one, 0)


def on_device(density, velocity, energy, material, limiter, owners, dest_tile, tile_shift):
    planes, rows, cols = density.shape
    assert planes == 1 and rows == TILE and cols == 2 * TILE
    gx, gy = lax.axis_size("gx"), lax.axis_size("gy")
    f32 = jnp.float32
    vmem = pl.BlockSpec(memory_space=pltpu.VMEM)
    shape = jax.ShapeDtypeStruct

    low3 = pl.BlockSpec((1, 8, cols), lambda i: (0, 0, 0))
    low4 = pl.BlockSpec((2, 1, 8, cols), lambda i: (0, 0, 0, 0))
    last = rows // 8 - 1
    high3 = pl.BlockSpec((1, 8, cols), lambda i: (0, last, 0))
    high4 = pl.BlockSpec((2, 1, 8, cols), lambda i: (0, 0, last, 0))
    halo_spec = pl.BlockSpec((8, cols), lambda i: (0, 0))
    near, far = pl.pallas_call(
        halo_kernel,
        grid=(1,),
        in_specs=[low3, low4, low3, low3, high3, high4, high3, high3],
        out_specs=[halo_spec, halo_spec],
        out_shape=[shape((8, cols), f32)] * 2,
        name="halo",
    )(density, velocity, energy, material, density, velocity, energy, material)
    near = lax.ppermute(near, "gy", near_pairs(gy))
    far = lax.ppermute(far, "gy", far_pairs(gy, False))

    message = shape((4 * rows + (RAW + 1) * EDGE, TILE), f32)
    field, first, second, edge = pl.pallas_call(
        functools.partial(block_kernel, step=8),
        in_specs=[vmem] * 8,
        out_specs=[vmem] * 4,
        out_shape=[
            shape((4, rows, cols), f32),
            message,
            message,
            shape((2 * (RAW + 1) * EDGE, TILE), f32),
        ],
        scratch_shapes=[
            pltpu.VMEM((4, 2, rows + 16, TILE), f32),
            pltpu.VMEM((2, 2, rows + 8, TILE), f32),
            pltpu.VMEM((2, 2, rows, TILE), f32),
            pltpu.VMEM((TILE, TILE), f32),
            pltpu.VMEM((rows, TILE), f32),
        ],
        name="block",
    )(density, velocity, energy, material, limiter, tile_shift, near, far)
    first = lax.ppermute(first, "gx", near_pairs(gx))
    second = lax.ppermute(second, "gx", far_pairs(gx, True))

    return pl.pallas_call(
        functools.partial(merge_kernel, step=8),
        in_specs=[vmem] * 6,
        out_specs=vmem,
        out_shape=shape((4, planes, rows, cols), f32),
        scratch_shapes=[pltpu.VMEM((rows, TILE), f32)],
        name="merge",
    )(field, edge, first, second, tile_shift, owners.reshape(-1, TILE))


def solution(mesh):
    assert mesh.shape["gx"] % 2 == 0 and mesh.shape["gy"] % 2 == 0
    placed = (
        P(None, "gy", "gx"),
        P(None, None, "gy", "gx"),
        P(None, "gy", "gx"),
        P(None, "gy", "gx"),
        P(None, "gy", "gx"),
        P(("gx", "gy")),
        P(("gx", "gy")),
        P(None, "gy"),
    )
    return jax.shard_map(
        on_device, mesh=mesh, in_specs=placed, out_specs=P(None, None, "gy", "gx"), check_vma=False
    )
```

```python
import functools

import jax
import jax.numpy as jnp
from jax import lax
from jax.experimental import pallas as pl
from jax.experimental.pallas import tpu as pltpu
from jax.sharding import PartitionSpec as P

TILE = 128
time_step = 0.05
STEP = 8
BLOCK = (4, 4, 4)
MERGE = 4
CHUNK = 32
VMEM_LIMIT = 8 << 20
EDGE = 8
RAW = 6


def near_pairs(count):
    return [(i, i ^ 1) for i in range(count)]


def far_pairs(count):
    pairs = []
    for i in range(1, count, 2):
        pairs += [(i, (i + 1) % count), ((i + 1) % count, i)]
    return pairs


def acoustic(density, energy, material):
    first, second = material == 0, material == 1
    less_one = jnp.where(first, 0.4, jnp.where(second, 2.0 / 3.0, 2.0)).astype(jnp.float32)
    both = jnp.where(first, 1.4 * 0.4, jnp.where(second, 10.0 / 9.0, 6.0)).astype(jnp.float32)
    return density * jnp.sqrt(both * energy), less_one * density * energy


def column_sums(impedance, pressure, speed_x, speed_y, from_left):
    along_x, along_y = impedance * speed_x, impedance * speed_y
    up, down = along_y + pressure, along_y - pressure
    return (
        from_left(impedance) + impedance,
        from_left(along_x + pressure) + (along_x - pressure),
        from_left(up) + up,
        from_left(down) + down,
    )


def nodes(below, above):
    scale = 1.0 / (below[0] + above[0])
    return (below[1] + above[1]) * scale, (below[2] + above[3]) * scale


def cell_values(impedance, pressure, speed_x, speed_y, density, energy, lower, upper, from_right):
    side_x = lower[0] + upper[0]
    side_y = lower[1] + upper[1]
    rise_y = upper[1] - lower[1]
    square = lower[0] * lower[0] + upper[0] * upper[0] + lower[1] * lower[1] + upper[1] * upper[1]
    far_x = from_right(side_x)
    sum_x = side_x + far_x
    sum_y = side_y + from_right(side_y)
    half_z = (0.5 * time_step) * impedance
    volume = (far_x - side_x) + (rise_y + from_right(rise_y))
    relaxation = (square + from_right(square)) - speed_x * sum_x - speed_y * sum_y
    left = (0.5 * time_step) * side_x
    right = (0.5 * time_step) * far_x
    scale = 1.0 / (1.0 + (right - left))
    total = density * (energy + 0.5 * (speed_x * speed_x + speed_y * speed_y))
    values = (
        density * scale,
        (density * speed_x + half_z * (sum_x - 4.0 * speed_x)) * scale,
        (density * speed_y + half_z * (sum_y - 4.0 * speed_y)) * scale,
        (total + (half_z * relaxation - (0.5 * time_step) * pressure * volume)) * scale,
    )
    return values, left, right


def remap_weights(shift, left, right):
    start = shift + left
    stop = 1.0 + shift + right
    centre = 0.5 * (start + stop)
    low_own, high_own = jnp.maximum(start, 0.0), jnp.minimum(stop, 1.0)
    span_own = jnp.maximum(high_own - low_own, 0.0)
    low_next, high_next = jnp.maximum(start, 1.0), jnp.minimum(stop, 2.0)
    span_next = jnp.maximum(high_next - low_next, 0.0)
    return (
        span_own,
        span_own * (0.5 * (high_own + low_own) - centre),
        span_next,
        span_next * (0.5 * (high_next + low_next) - centre),
    )


def remapped_field(value, steepness, weights, from_left, from_right):
    back = value - from_left(value)
    fore = from_right(back)
    mean = 0.5 * (back + fore)
    rising = jnp.maximum(jnp.minimum(steepness * jnp.minimum(back, fore), mean), 0.0)
    falling = jnp.minimum(jnp.maximum(steepness * jnp.maximum(back, fore), mean), 0.0)
    slope = rising + falling
    own = weights[0] * value + weights[1] * slope
    return own + from_left(weights[2] * value + weights[3] * slope)


class Wide:
    def __init__(self, parts):
        self.parts = tuple(parts)

    def _with(self, other, op):
        if isinstance(other, Wide):
            return Wide(op(a, b) for a, b in zip(self.parts, other.parts))
        return Wide(op(a, other) for a in self.parts)

    def __add__(self, o):
        return self._with(o, lambda a, b: a + b)

    def __radd__(self, o):
        return self._with(o, lambda a, b: b + a)

    def __sub__(self, o):
        return self._with(o, lambda a, b: a - b)

    def __mul__(self, o):
        return self._with(o, lambda a, b: a * b)

    def __rmul__(self, o):
        return self._with(o, lambda a, b: b * a)


def wide_left(lane, parts):
    turned = [pltpu.roll(a, 1, 1) for a in parts]
    return [turned[0]] + [
        jnp.where(lane == 0, turned[i - 1], turned[i]) for i in range(1, len(turned))
    ]


def wide_right(lane, parts):
    width = parts[0].shape[-1]
    turned = [pltpu.roll(a, width - 1, 1) for a in parts]
    return [
        jnp.where(lane == width - 1, turned[i + 1], turned[i]) for i in range(len(turned) - 1)
    ] + [turned[-1]]


def cut(array, h):
    return array[:, h * TILE : (h + 1) * TILE]


def lanes(h):
    return slice(h * TILE, (h + 1) * TILE)


def block_kernel(
    rho_hbm, vel_hbm, en_hbm, mat_hbm, lim_hbm, shift_hbm, owner_hbm,
    out_ref, first_ref, second_ref, edge_ref, rim_ref, near_ref, far_ref, row_ref,
    rho_ref, vel_ref, en_ref, mat_ref, lim_ref, shift_ref, owner_ref,
    sums_ref, node_ref, press_ref, shifts_ref, edges_ref, sems, small_sems,
):
    rows, cols = rho_ref.shape
    halves = range(cols // TILE)
    last = len(halves) - 1
    even_x = lax.axis_index("gx") % 2 == 0
    even_y = lax.axis_index("gy") % 2 == 0
    pad = 8
    chunks, inner = rows // CHUNK, CHUNK // STEP

    def copies(c):
        part = pl.ds(pl.multiple_of(c * CHUNK, CHUNK), CHUNK)
        return [
            pltpu.make_async_copy(rho_hbm.at[0, part, :], rho_ref.at[part, :], sems.at[0, c]),
            pltpu.make_async_copy(en_hbm.at[0, part, :], en_ref.at[part, :], sems.at[1, c]),
            pltpu.make_async_copy(mat_hbm.at[0, part, :], mat_ref.at[part, :], sems.at[2, c]),
            pltpu.make_async_copy(vel_hbm.at[:, 0, part, :], vel_ref.at[:, part, :], sems.at[3, c]),
            pltpu.make_async_copy(lim_hbm.at[0, part, :], lim_ref.at[part, :], sems.at[4, c]),
        ]

    for c in range(chunks):
        for copy in copies(c):
            copy.start()

    small = [
        pltpu.make_async_copy(shift_hbm, shift_ref, small_sems.at[0]),
        pltpu.make_async_copy(owner_hbm, owner_ref, small_sems.at[1]),
    ]
    for copy in small:
        copy.start()
    lane = lax.broadcasted_iota(jnp.int32, (STEP, TILE), 1)
    left = lambda a: Wide(wide_left(lane, a.parts))
    right = lambda a: Wide(wide_right(lane, a.parts))

    def at_rows(i, offset=0):
        return pl.ds(pl.multiple_of(i * STEP, STEP) + offset, STEP)

    def first_pass(i, _):
        here = at_rows(i)
        rho = [rho_ref[here, lanes(h)] for h in halves]
        en = [en_ref[here, lanes(h)] for h in halves]
        mat = [mat_ref[here, lanes(h)] for h in halves]
        sx = [vel_ref[0, here, lanes(h)] for h in halves]
        sy = [vel_ref[1, here, lanes(h)] for h in halves]
        both = [acoustic(rho[h], en[h], mat[h]) for h in halves]
        z, p = [b[0] for b in both], [b[1] for b in both]
        for h in halves:
            press_ref[0, h, here, :] = z[h]
            press_ref[1, h, here, :] = p[h]
        totals = column_sums(Wide(z), Wide(p), Wide(sx), Wide(sy), left)
        for s, total in enumerate(totals):
            for h in halves:
                sums_ref[s, h, at_rows(i, pad), :] = total.parts[h]
        lim = [lim_ref[here, lanes(h)].astype(jnp.float32) for h in (0, last)]
        mats = [mat[0].astype(jnp.float32), mat[-1].astype(jnp.float32)]
        edge = jnp.zeros((STEP, TILE), jnp.float32)
        ends = ((rho[0], rho[-1]), (sx[0], sx[-1]), (sy[0], sy[-1]), (en[0], en[-1]), mats, lim)
        for k, (start, stop) in enumerate(ends):
            turned = pltpu.roll(jnp.where(lane < TILE // 2, start, stop), (2 * k + 1) * EDGE, 1)
            edge = jnp.where(lane >= 2 * k * EDGE, turned, edge)
        edges_ref[here, :] = edge
        return 0

    def first_chunk(c, _):
        for copy in copies(c):
            copy.wait()
        step = lambda j, _: first_pass(c * inner + j, 0)
        return lax.fori_loop(0, inner, step, 0, unroll=BLOCK[0])

    for s in range(4):
        for h in halves:
            sums_ref[s, h, 0:pad, :] = jnp.full((pad, TILE), float(s == 0), jnp.float32)
            sums_ref[s, h, rows + pad :, :] = jnp.full((pad, TILE), float(s == 0), jnp.float32)
    lax.fori_loop(0, chunks, first_chunk, 0)

    def second_pass(i, _):
        for h in halves:
            under = [sums_ref[s, h, at_rows(i, pad - 1), :] for s in range(3)]
            over = [sums_ref[s, h, at_rows(i, pad), :] for s in (0, 1, 3)]
            nx, ny = nodes(under, [over[0], over[1], None, over[2]])
            node_ref[0, h, at_rows(i), :] = nx
            node_ref[1, h, at_rows(i), :] = ny
        return 0

    for copy in small:
        copy.wait()
    shifts_ref[...] = jnp.broadcast_to(shift_ref[...], (TILE, TILE)).T
    column, count = lax.axis_index("gx"), lax.axis_size("gx")
    owner = owner_ref[...]
    row_ref[0:1, :] = shift_ref[...]
    for k, which in enumerate(((column + count - 1) % count, (column + 1) % count)):
        hits = jnp.where(owner == which, 1.0, 0.0)
        total = jnp.sum(jnp.sum(hits, axis=1, keepdims=True), axis=0, keepdims=True)
        row_ref[k + 1 : k + 2, :] = jnp.broadcast_to(total, (1, TILE))
    lax.fori_loop(0, rows // STEP, second_pass, 0, unroll=BLOCK[1])
    for h in halves:
        for d in range(2):
            node_ref[d, h, rows : rows + STEP, :] = jnp.zeros((STEP, TILE), jnp.float32)

    for k in range(4):
        for h in halves:
            pick = lambda row: (
                press_ref[k, h, row : row + 1, :]
                if k < 2
                else vel_ref[k - 2, row : row + 1, lanes(h)]
            )
            top, bottom = pick(rows - 1), pick(0)
            near_ref[k : k + 1, lanes(h)] = jnp.where(even_y, top, bottom)
            far_ref[k : k + 1, lanes(h)] = jnp.where(even_y, bottom, top)
    for r, row in enumerate((0, rows - 1)):
        at, to = slice(row, row + 1), slice(r, r + 1)
        joint = slice(1, 2) if r == 0 else slice(rows - 1, rows)
        for h in halves:
            kept = [
                press_ref[0, h, at, :], press_ref[1, h, at, :],
                vel_ref[0, at, lanes(h)], vel_ref[1, at, lanes(h)],
                rho_ref[at, lanes(h)], en_ref[at, lanes(h)],
                lim_ref[at, lanes(h)].astype(jnp.float32), shifts_ref[at, :],
                *(sums_ref[s, h, pad + row : pad + row + 1, :] for s in range(4)),
                *(node_ref[d, h, joint, :] for d in range(2)),
            ]
            for k, value in enumerate(kept):
                rim_ref[k, to, lanes(h)] = value

    edge_ref[...] = edges_ref[...].T[0 : 2 * RAW * EDGE, :]

    def third_pass(i, _):
        here = at_rows(i)
        wide = lambda ref, *at: Wide(ref[(*at, here, lanes(h))] for h in halves)
        rho, en = wide(rho_ref), wide(en_ref)
        sx, sy = wide(vel_ref, 0), wide(vel_ref, 1)
        z = Wide(press_ref[0, h, here, :] for h in halves)
        p = Wide(press_ref[1, h, here, :] for h in halves)
        lower = [Wide(node_ref[d, h, here, :] for h in halves) for d in range(2)]
        upper = [Wide(node_ref[d, h, at_rows(i, 1), :] for h in halves) for d in range(2)]
        steepness = Wide(lim_ref[here, lanes(h)].astype(jnp.float32) + 1.0 for h in halves)
        shift = shifts_ref[here, :]
        values, dl, dr = wide_cells(z, p, sx, sy, rho, en, lower, upper, right)
        weights = [remap_weights(shift, dl.parts[h], dr.parts[h]) for h in halves]
        weights = [Wide(w) for w in zip(*weights)]
        for f, value in enumerate(values):
            done = wide_field(value, steepness, weights, left, right)
            for h in halves:
                out_ref[f, here, lanes(h)] = done.parts[h]
            ends = done.parts[0], done.parts[-1]
            spot = pl.ds(pl.multiple_of(f * rows + i * STEP, STEP), STEP)
            first_ref[spot, :] = jnp.where(even_x, ends[1], ends[0])
            second_ref[spot, :] = jnp.where(even_x, ends[0], ends[1])
        return 0

    lax.fori_loop(0, rows // STEP, third_pass, 0, unroll=BLOCK[2])


def rim_kernel(near_ref, far_ref, kept_ref, edge_ref, rows_ref, first_ref, second_ref, corner_ref):
    cols = near_ref.shape[-1]
    halves = range(cols // TILE)
    even_x = lax.axis_index("gx") % 2 == 0
    level, levels = lax.axis_index("gy"), lax.axis_size("gy")
    even_y = level % 2 == 0
    near, far = near_ref[0:4, :], far_ref[0:4, :]
    below = jnp.where(level == 0, 0.0, jnp.where(even_y, far, near))
    above = jnp.where(level == levels - 1, 0.0, jnp.where(even_y, near, far))

    lane = lax.broadcasted_iota(jnp.int32, (8, TILE), 1)
    bottom = lax.broadcasted_iota(jnp.int32, (8, TILE), 0) == 0
    left = lambda a: Wide(wide_left(lane, a.parts))
    right = lambda a: Wide(wide_right(lane, a.parts))

    kept = [Wide(kept_ref[k, :, lanes(h)] for h in halves) for k in range(14)]
    z, p, sx, sy, rho, en, lim, shift = kept[:8]
    own, joint = kept[8:12], kept[12:14]
    outer = [
        Wide(jnp.where(bottom, cut(below[k : k + 1, :], h), cut(above[k : k + 1, :], h)) for h in halves)
        for k in range(4)
    ]
    outer = column_sums(*outer, left)
    under, over = [], []
    for a, b in zip(outer, own):
        under.append(Wide(jnp.where(bottom, x, y) for x, y in zip(a.parts, b.parts)))
        over.append(Wide(jnp.where(bottom, y, x) for x, y in zip(a.parts, b.parts)))
    fresh = [nodes([q.parts[h] for q in under], [q.parts[h] for q in over]) for h in halves]
    fresh = [Wide(q) for q in zip(*fresh)]
    lower = [Wide(jnp.where(bottom, x, y) for x, y in zip(a.parts, b.parts)) for a, b in zip(fresh, joint)]
    upper = [Wide(jnp.where(bottom, y, x) for x, y in zip(a.parts, b.parts)) for a, b in zip(fresh, joint)]
    values, dl, dr = wide_cells(z, p, sx, sy, rho, en, lower, upper, right)
    weights = [remap_weights(shift.parts[h], dl.parts[h], dr.parts[h]) for h in halves]
    weights = [Wide(w) for w in zip(*weights)]
    steepness = Wide(q + 1.0 for q in lim.parts)
    for f, value in enumerate(values):
        done = wide_field(value, steepness, weights, left, right)
        for h in halves:
            rows_ref[2 * f : 2 * f + 2, lanes(h)] = done.parts[h][0:2, :]
        ends = done.parts[0][0:2, :], done.parts[-1][0:2, :]
        first_ref[2 * f : 2 * f + 2, :] = jnp.where(even_x, ends[1], ends[0])
        second_ref[2 * f : 2 * f + 2, :] = jnp.where(even_x, ends[0], ends[1])

    halo = jnp.concatenate([below, above], axis=0)
    corner = pltpu.roll(jnp.where(lane < TILE // 2, cut(halo, 0), cut(halo, len(halves) - 1)), EDGE, 1)
    corner = jnp.concatenate([corner, jnp.zeros((TILE - 8, TILE), jnp.float32)], axis=0)
    corner_t = corner.T[0 : 2 * EDGE, :]
    corner_ref[...] = corner_t
    for k in range(RAW + 1):
        at = 2 * k * EDGE
        if k < RAW:
            right_edge, left_edge = edge_ref[at : at + EDGE, :], edge_ref[at + EDGE : at + 2 * EDGE, :]
        else:
            right_edge, left_edge = corner_t[0:EDGE, :], corner_t[EDGE:, :]
        spot = slice(8 + k * EDGE, 8 + (k + 1) * EDGE)
        first_ref[spot, :] = jnp.where(even_x, right_edge, left_edge)
        second_ref[spot, :] = jnp.where(even_x, left_edge, right_edge)


def edge_kernel(edge_ref, corner_ref, first_ref, second_ref, row_ref, patch_ref):
    rows = patch_ref.shape[0]
    even_x = lax.axis_index("gx") % 2 == 0
    span = 4 * EDGE

    def window(k):
        spot = slice(8 + k * EDGE, 8 + (k + 1) * EDGE)
        from_near, from_far = first_ref[spot, :], second_ref[spot, :]
        own, at = (edge_ref, 2 * k * EDGE) if k < RAW else (corner_ref, 0)
        return jnp.concatenate(
            [
                jnp.where(even_x, from_far, from_near),
                own[at + EDGE : at + 2 * EDGE, :],
                own[at : at + EDGE, :],
                jnp.where(even_x, from_near, from_far),
            ],
            axis=0,
        )

    left = lambda a: pltpu.roll(a, 1, 0)
    right = lambda a: pltpu.roll(a, span - 1, 0)
    rho, sx, sy, en, mat, lim = (window(k) for k in range(RAW))
    halo = window(RAW)
    z, p = acoustic(rho, en, mat)
    own = column_sums(z, p, sx, sy, left)
    spread = lambda k: jnp.broadcast_to(halo[:, k : k + 1], (span, rows))
    below = column_sums(*(spread(k) for k in range(4)), left)
    above = column_sums(*(spread(k) for k in range(4, 8)), left)
    lane = lax.broadcasted_iota(jnp.int32, (span, rows), 1)
    under = [jnp.where(lane == 0, b, pltpu.roll(a, 1, 1)) for a, b in zip(own, below)]
    over = [jnp.where(lane == rows - 1, b, pltpu.roll(a, rows - 1, 1)) for a, b in zip(own, above)]
    values, dl, dr = cell_values(
        z, p, sx, sy, rho, en, nodes(under, own), nodes(own, over), right
    )
    weights = remap_weights(row_ref[0:1, :], dl, dr)
    fields = [remapped_field(v, lim + 1.0, weights, left, right) for v in values]
    patch_ref[...] = jnp.concatenate(fields, axis=0).T


def merge_kernel(
    field_ref, rows_ref, first_ref, second_ref, small_first_ref, small_second_ref, patch_ref,
    row_ref, out_hbm, out_ref, sems,
):
    rows = field_ref.shape[1]
    even_x = lax.axis_index("gx") % 2 == 0
    span = 4 * EDGE
    chunks, inner = rows // CHUNK, CHUNK // STEP

    to_left, to_right = row_ref[1:2, :], row_ref[2:3, :]

    def put(here, row, patch, pick_own, pick_sent):
        goes_left, goes_right = row < to_left, row >= rows - to_right
        lane = lax.broadcasted_iota(jnp.int32, patch.shape, 1)
        head, tail = lane < 3, lane >= TILE - 2
        for f in range(4):
            at_left = pltpu.roll(patch, (-(span * f + EDGE)) % TILE, 1)
            at_right = pltpu.roll(patch, (-(span * f + 3 * EDGE)) % TILE, 1)
            from_near, from_far = pick_sent(f)
            own_0 = jnp.where(head, at_left, pick_own(f, 0))
            own_1 = jnp.where(tail, at_right, pick_own(f, 1))
            left_tile = jnp.where(tail, at_left, jnp.where(even_x, from_far, from_near))
            right_tile = jnp.where(head, at_right, jnp.where(even_x, from_near, from_far))
            out_ref[f, here, lanes(0)] = jnp.where(
                goes_right, left_tile, jnp.where(goes_left, own_1, own_0)
            )
            out_ref[f, here, lanes(1)] = jnp.where(
                goes_right, own_0, jnp.where(goes_left, right_tile, own_1)
            )

    row_in = lax.broadcasted_iota(jnp.int32, (STEP, TILE), 0)

    def one(i, _):
        here = pl.ds(pl.multiple_of(i * STEP, STEP), STEP)

        def sent(f):
            spot = pl.ds(pl.multiple_of(f * rows + i * STEP, STEP), STEP)
            return first_ref[spot, :], second_ref[spot, :]

        row = (row_in + i * STEP).astype(jnp.float32)
        put(here, row, patch_ref[here, :], lambda f, h: field_ref[f, here, lanes(h)], sent)
        return 0

    def rim(r):
        row = r * (rows - 1)
        here = slice(row, row + 1)

        def sent(f):
            spot = slice(2 * f + r, 2 * f + r + 1)
            return small_first_ref[spot, :], small_second_ref[spot, :]

        own = lambda f, h: rows_ref[2 * f + r : 2 * f + r + 1, lanes(h)]
        put(here, jnp.full((1, TILE), float(row)), patch_ref[here, :], own, sent)

    def copy(c):
        part = pl.ds(pl.multiple_of(c * CHUNK, CHUNK), CHUNK)
        return pltpu.make_async_copy(out_ref.at[:, part, :], out_hbm.at[:, 0, part, :], sems.at[c])

    def chunk(c, _):
        lax.fori_loop(0, inner, lambda j, _: one(c * inner + j, 0), 0, unroll=MERGE)
        pl.when(c == 0)(lambda: rim(0))
        pl.when(c == chunks - 1)(lambda: rim(1))
        copy(c).start()
        return 0

    lax.fori_loop(0, chunks, chunk, 0)
    for c in range(chunks):
        copy(c).wait()


def on_device(density, velocity, energy, material, limiter, owners, dest_tile, tile_shift):
    planes, rows, cols = density.shape
    assert planes == 1 and rows == TILE and cols == 2 * TILE
    gx, gy = lax.axis_size("gx"), lax.axis_size("gy")
    f32 = jnp.float32
    vmem = pl.BlockSpec(memory_space=pltpu.VMEM)
    hbm = pl.BlockSpec(memory_space=pltpu.HBM)
    shape = lambda *dims: jax.ShapeDtypeStruct(dims, f32)
    params = pltpu.CompilerParams(vmem_limit_bytes=VMEM_LIMIT)
    chunks = rows // CHUNK
    stay = lambda array: pltpu.with_memory_space_constraint(array, pltpu.HBM)

    field, first, second, edge, kept, near, far, per_row = pl.pallas_call(
        block_kernel,
        in_specs=[hbm] * 7,
        out_specs=[vmem] * 8,
        out_shape=[
            shape(4, rows, cols),
            shape(4 * rows, TILE),
            shape(4 * rows, TILE),
            shape(2 * RAW * EDGE, TILE),
            shape(14, 8, cols),
            shape(8, cols),
            shape(8, cols),
            shape(8, TILE),
        ],
        scratch_shapes=[
            pltpu.VMEM((rows, cols), f32),
            pltpu.VMEM((2, rows, cols), f32),
            pltpu.VMEM((rows, cols), f32),
            pltpu.VMEM((rows, cols), jnp.int32),
            pltpu.VMEM((rows, cols), jnp.int32),
            pltpu.VMEM((1, rows), f32),
            pltpu.VMEM((rows * cols // TILE // TILE, TILE), jnp.int32),
            pltpu.VMEM((4, 2, rows + 16, TILE), f32),
            pltpu.VMEM((2, 2, rows + 8, TILE), f32),
            pltpu.VMEM((2, 2, rows, TILE), f32),
            pltpu.VMEM((TILE, TILE), f32),
            pltpu.VMEM((rows, TILE), f32),
            pltpu.SemaphoreType.DMA((5, chunks)),
            pltpu.SemaphoreType.DMA((2,)),
        ],
        compiler_params=params,
        name="block",
    )(*map(stay, (density, velocity, energy, material, limiter, tile_shift, owners.reshape(-1, TILE))))
    first = lax.ppermute(first, "gx", near_pairs(gx))
    near = lax.ppermute(near, "gy", near_pairs(gy))
    far = lax.ppermute(far, "gy", far_pairs(gy))
    second = lax.ppermute(second, "gx", far_pairs(gx))

    small = shape(8 + (RAW + 1) * EDGE, TILE)
    outer_rows, small_first, small_second, corner = pl.pallas_call(
        rim_kernel,
        in_specs=[vmem] * 4,
        out_specs=[vmem] * 4,
        out_shape=[shape(8, cols), small, small, shape(2 * EDGE, TILE)],
        compiler_params=params,
        name="rim",
    )(near, far, kept, edge)
    small_first = lax.ppermute(small_first, "gx", near_pairs(gx))
    small_second = lax.ppermute(small_second, "gx", far_pairs(gx))

    patch = pl.pallas_call(
        edge_kernel,
        in_specs=[vmem] * 5,
        out_specs=vmem,
        out_shape=shape(rows, TILE),
        compiler_params=params,
        name="edge",
    )(edge, corner, small_first, small_second, per_row)

    return pl.pallas_call(
        merge_kernel,
        in_specs=[vmem] * 8,
        out_specs=hbm,
        out_shape=shape(4, planes, rows, cols),
        scratch_shapes=[pltpu.VMEM((4, rows, cols), f32), pltpu.SemaphoreType.DMA((chunks,))],
        compiler_params=params,
        name="merge",
    )(
        field, outer_rows, first, second, small_first, small_second, patch, per_row,
    )


def wide_cells(z, p, sx, sy, rho, en, lower, upper, from_right):
    halves = range(len(z.parts))
    pieces = []
    for h in halves:
        lx, ly, ux, uy = (q.parts[h] for q in (*lower, *upper))
        pieces.append((lx + ux, ly + uy, uy - ly, lx * lx + ux * ux + ly * ly + uy * uy))
    far = [from_right(Wide(q)).parts for q in zip(*pieces)]
    results = []
    for h in halves:
        queue = [far[k][h] for k in (0, 1, 2, 3)]
        order = iter(queue)
        results.append(
            cell_values(
                z.parts[h], p.parts[h], sx.parts[h], sy.parts[h], rho.parts[h], en.parts[h],
                [q.parts[h] for q in lower], [q.parts[h] for q in upper], lambda _: next(order),
            )
        )
    values = [Wide(results[h][0][f] for h in halves) for f in range(4)]
    return values, Wide(r[1] for r in results), Wide(r[2] for r in results)


def wide_field(value, steepness, weights, left, right):
    back = value - left(value)
    fore = right(back)
    owns, nexts = [], []
    for h in range(len(value.parts)):
        b, f, k = back.parts[h], fore.parts[h], steepness.parts[h]
        mean = 0.5 * (b + f)
        rising = jnp.maximum(jnp.minimum(k * jnp.minimum(b, f), mean), 0.0)
        falling = jnp.minimum(jnp.maximum(k * jnp.maximum(b, f), mean), 0.0)
        slope = rising + falling
        w = [q.parts[h] for q in weights]
        owns.append(w[0] * value.parts[h] + w[1] * slope)
        nexts.append(w[2] * value.parts[h] + w[3] * slope)
    return Wide(owns) + left(Wide(nexts))


def solution(mesh):
    assert mesh.shape["gx"] % 2 == 0 and mesh.shape["gy"] % 2 == 0
    placed = (
        P(None, "gy", "gx"),
        P(None, None, "gy", "gx"),
        P(None, "gy", "gx"),
        P(None, "gy", "gx"),
        P(None, "gy", "gx"),
        P(("gx", "gy")),
        P(("gx", "gy")),
        P(None, "gy"),
    )
    return jax.shard_map(
        on_device, mesh=mesh, in_specs=placed, out_specs=P(None, None, "gy", "gx"), check_vma=False
    )
```

```python
import jax
import jax.numpy as jnp
from jax import lax
from jax.experimental import pallas as pl
from jax.experimental.pallas import tpu as pltpu
from jax.sharding import PartitionSpec as P


TILE = 128
time_step = 0.05
STEP = 8
BLOCK = (4, 4, 8, 8)
MERGE = 4
CHUNK = 32
VMEM_LIMIT = 8 << 20
EDGE = 8
RAW = 6


def near_pairs(count):
    return [(i, i ^ 1) for i in range(count)]


def far_pairs(count):
    pairs = []
    for i in range(1, count, 2):
        pairs += [(i, (i + 1) % count), ((i + 1) % count, i)]
    return pairs


def acoustic(density, energy, material):
    first, second = material == 0, material == 1
    less_one = jnp.where(first, 0.4, jnp.where(second, 2.0 / 3.0, 2.0)).astype(jnp.float32)
    both = jnp.where(first, 1.4 * 0.4, jnp.where(second, 10.0 / 9.0, 6.0)).astype(jnp.float32)
    return density * jnp.sqrt(both * energy), less_one * density * energy


def column_sums(impedance, pressure, speed_x, speed_y, from_left):
    along_x, along_y = impedance * speed_x, impedance * speed_y
    up, down = along_y + pressure, along_y - pressure
    return (
        from_left(impedance) + impedance,
        from_left(along_x + pressure) + (along_x - pressure),
        from_left(up) + up,
        from_left(down) + down,
    )


def nodes(below, above):
    scale = 1.0 / (below[0] + above[0])
    return (below[1] + above[1]) * scale, (below[2] + above[3]) * scale


def cell_update(impedance, pressure, speed_x, speed_y, density, energy, lower, upper, from_right):
    side_x = lower[0] + upper[0]
    side_y = lower[1] + upper[1]
    rise_y = upper[1] - lower[1]
    square = lower[0] * lower[0] + upper[0] * upper[0] + lower[1] * lower[1] + upper[1] * upper[1]
    far_x = from_right(side_x)
    sum_x = side_x + far_x
    sum_y = side_y + from_right(side_y)
    half_z = (0.5 * time_step) * impedance
    volume = (far_x - side_x) + (rise_y + from_right(rise_y))
    relaxation = (square + from_right(square)) - speed_x * sum_x - speed_y * sum_y
    left = (0.5 * time_step) * side_x
    right = (0.5 * time_step) * far_x
    total = density * (energy + 0.5 * (speed_x * speed_x + speed_y * speed_y))
    conserved = (
        density,
        density * speed_x + half_z * (sum_x - 4.0 * speed_x),
        density * speed_y + half_z * (sum_y - 4.0 * speed_y),
        total + (half_z * relaxation - (0.5 * time_step) * pressure * volume),
    )
    return conserved, 0.5 / (1.0 + (right - left)), left, right


def next_weights(shift, left, right):
    start = shift + left
    stop = (1.0 + shift) + right
    low = jnp.maximum(start, 1.0)
    span = jnp.maximum(stop - low, 0.0)
    return 2.0 * span, (0.5 * span) * (low - start)


def limited(back, fore, twice):
    low = jnp.minimum(twice * jnp.maximum(back, fore), 0.0)
    high = jnp.maximum(twice * jnp.minimum(back, fore), 0.0)
    return jnp.minimum(jnp.maximum(back + fore, low), high)


def remapped_field(conserved, scale, twice, weights, from_left, from_right):
    half = conserved * scale
    back = half - from_left(half)
    slope = limited(back, from_right(back), twice)
    onward = weights[0] * half + weights[1] * slope
    return (conserved - onward) + from_left(onward)


class Wide:
    def __init__(self, parts):
        self.parts = tuple(parts)

    def _with(self, other, op):
        if isinstance(other, Wide):
            return Wide(op(a, b) for a, b in zip(self.parts, other.parts))
        return Wide(op(a, other) for a in self.parts)

    def __add__(self, o):
        return self._with(o, lambda a, b: a + b)

    def __radd__(self, o):
        return self._with(o, lambda a, b: b + a)

    def __sub__(self, o):
        return self._with(o, lambda a, b: a - b)

    def __mul__(self, o):
        return self._with(o, lambda a, b: a * b)

    def __rmul__(self, o):
        return self._with(o, lambda a, b: b * a)


def wide_left(lane, parts):
    turned = [pltpu.roll(a, 1, 1) for a in parts]
    return [turned[0]] + [
        jnp.where(lane == 0, turned[i - 1], turned[i]) for i in range(1, len(turned))
    ]


def wide_right(lane, parts):
    width = parts[0].shape[-1]
    turned = [pltpu.roll(a, width - 1, 1) for a in parts]
    return [
        jnp.where(lane == width - 1, turned[i + 1], turned[i]) for i in range(len(turned) - 1)
    ] + [turned[-1]]


def cut(array, h):
    return array[:, h * TILE : (h + 1) * TILE]


def lanes(h):
    return slice(h * TILE, (h + 1) * TILE)


def wide_cells(z, p, sx, sy, rho, en, lower, upper, from_right):
    parts = range(len(z.parts))
    pieces = []
    for h in parts:
        lx, ly, ux, uy = (q.parts[h] for q in (*lower, *upper))
        pieces.append((lx + ux, ly + uy, uy - ly, lx * lx + ux * ux + ly * ly + uy * uy))
    far = [from_right(Wide(q)).parts for q in zip(*pieces)]
    results = []
    for h in parts:
        order = iter([far[k][h] for k in range(4)])
        results.append(
            cell_update(
                z.parts[h], p.parts[h], sx.parts[h], sy.parts[h], rho.parts[h], en.parts[h],
                [q.parts[h] for q in lower], [q.parts[h] for q in upper], lambda _: next(order),
            )
        )
    return results


def wide_field(conserved, scale, twice, weights, left, right):
    half = conserved * scale
    back = half - left(half)
    fore = right(back)
    onward = []
    for h in range(len(half.parts)):
        slope = limited(back.parts[h], fore.parts[h], twice.parts[h])
        onward.append(weights[0].parts[h] * half.parts[h] + weights[1].parts[h] * slope)
    onward = Wide(onward)
    return (conserved - onward) + left(onward)


def block_kernel(
    rho_hbm, vel_hbm, en_hbm, mat_hbm, lim_hbm, shift_hbm, owner_hbm,
    first_ref, second_ref, edge_ref, rim_ref, near_ref, far_ref, row_ref,
    rho_ref, vel_ref, en_ref, mat_ref, lim_ref, shift_ref, owner_ref,
    sums_ref, node_ref, press_ref, shifts_ref, edges_ref, kept_ref, sems, small_sems,
):
    rows, cols = rho_ref.shape
    halves = range(cols // TILE)
    last = len(halves) - 1
    even_x = lax.axis_index("gx") % 2 == 0
    even_y = lax.axis_index("gy") % 2 == 0
    pad = 8
    chunks, inner = rows // CHUNK, CHUNK // STEP

    def copies(c):
        part = pl.ds(pl.multiple_of(c * CHUNK, CHUNK), CHUNK)
        return [
            pltpu.make_async_copy(rho_hbm.at[0, part, :], rho_ref.at[part, :], sems.at[0, c]),
            pltpu.make_async_copy(en_hbm.at[0, part, :], en_ref.at[part, :], sems.at[1, c]),
            pltpu.make_async_copy(mat_hbm.at[0, part, :], mat_ref.at[part, :], sems.at[2, c]),
            pltpu.make_async_copy(vel_hbm.at[:, 0, part, :], vel_ref.at[:, part, :], sems.at[3, c]),
            pltpu.make_async_copy(lim_hbm.at[0, part, :], lim_ref.at[part, :], sems.at[4, c]),
        ]

    for c in range(chunks):
        for copy in copies(c):
            copy.start()

    small = [
        pltpu.make_async_copy(shift_hbm, shift_ref, small_sems.at[0]),
        pltpu.make_async_copy(owner_hbm, owner_ref, small_sems.at[1]),
    ]
    for copy in small:
        copy.start()
    lane = lax.broadcasted_iota(jnp.int32, (STEP, TILE), 1)
    left = lambda a: Wide(wide_left(lane, a.parts))
    right = lambda a: Wide(wide_right(lane, a.parts))

    def at_rows(i, offset=0):
        return pl.ds(pl.multiple_of(i * STEP, STEP) + offset, STEP)

    def first_pass(i):
        here = at_rows(i)
        rho = [rho_ref[here, lanes(h)] for h in halves]
        en = [en_ref[here, lanes(h)] for h in halves]
        mat = [mat_ref[here, lanes(h)] for h in halves]
        sx = [vel_ref[0, here, lanes(h)] for h in halves]
        sy = [vel_ref[1, here, lanes(h)] for h in halves]
        both = [acoustic(rho[h], en[h], mat[h]) for h in halves]
        z, p = [b[0] for b in both], [b[1] for b in both]
        for h in halves:
            press_ref[0, h, here, :] = z[h]
            press_ref[1, h, here, :] = p[h]
        totals = column_sums(Wide(z), Wide(p), Wide(sx), Wide(sy), left)
        for s, total in enumerate(totals):
            for h in halves:
                sums_ref[s, h, at_rows(i, pad), :] = total.parts[h]
        lim = [lim_ref[here, lanes(h)].astype(jnp.float32) for h in (0, last)]
        mats = [mat[0].astype(jnp.float32), mat[-1].astype(jnp.float32)]
        edge = jnp.zeros((STEP, TILE), jnp.float32)
        ends = ((rho[0], rho[-1]), (sx[0], sx[-1]), (sy[0], sy[-1]), (en[0], en[-1]), mats, lim)
        for k, (start, stop) in enumerate(ends):
            turned = pltpu.roll(jnp.where(lane < TILE // 2, start, stop), (2 * k + 1) * EDGE, 1)
            edge = jnp.where(lane >= 2 * k * EDGE, turned, edge)
        edges_ref[here, :] = edge
        return 0

    def first_chunk(c, _):
        for copy in copies(c):
            copy.wait()
        step = lambda j, _: first_pass(c * inner + j)
        return lax.fori_loop(0, inner, step, 0, unroll=BLOCK[0])

    for s in range(4):
        for h in halves:
            sums_ref[s, h, 0:pad, :] = jnp.full((pad, TILE), float(s == 0), jnp.float32)
            sums_ref[s, h, rows + pad :, :] = jnp.full((pad, TILE), float(s == 0), jnp.float32)
    lax.fori_loop(0, chunks, first_chunk, 0)

    def second_pass(i, _):
        for h in halves:
            under = [sums_ref[s, h, at_rows(i, pad - 1), :] for s in range(3)]
            over = [sums_ref[s, h, at_rows(i, pad), :] for s in (0, 1, 3)]
            nx, ny = nodes(under, [over[0], over[1], None, over[2]])
            node_ref[0, h, at_rows(i), :] = nx
            node_ref[1, h, at_rows(i), :] = ny
        return 0

    for copy in small:
        copy.wait()
    shifts_ref[...] = jnp.broadcast_to(shift_ref[...], (TILE, TILE)).T
    column, count = lax.axis_index("gx"), lax.axis_size("gx")
    owner = owner_ref[...]
    row_ref[0:1, :] = shift_ref[...]
    for k, which in enumerate(((column + count - 1) % count, (column + 1) % count)):
        hits = jnp.where(owner == which, 1.0, 0.0)
        total = jnp.sum(jnp.sum(hits, axis=1, keepdims=True), axis=0, keepdims=True)
        row_ref[k + 1 : k + 2, :] = jnp.broadcast_to(total, (1, TILE))
    lax.fori_loop(0, rows // STEP, second_pass, 0, unroll=BLOCK[1])
    for h in halves:
        for d in range(2):
            node_ref[d, h, rows : rows + STEP, :] = jnp.zeros((STEP, TILE), jnp.float32)

    for k in range(4):
        for h in halves:
            pick = lambda row: (
                press_ref[k, h, row : row + 1, :]
                if k < 2
                else vel_ref[k - 2, row : row + 1, lanes(h)]
            )
            top, bottom = pick(rows - 1), pick(0)
            near_ref[k : k + 1, lanes(h)] = jnp.where(even_y, top, bottom)
            far_ref[k : k + 1, lanes(h)] = jnp.where(even_y, bottom, top)
    for r, row in enumerate((0, rows - 1)):
        at, to = slice(row, row + 1), slice(r, r + 1)
        joint = slice(1, 2) if r == 0 else slice(rows - 1, rows)
        for h in halves:
            kept = [
                press_ref[0, h, at, :], press_ref[1, h, at, :],
                vel_ref[0, at, lanes(h)], vel_ref[1, at, lanes(h)],
                rho_ref[at, lanes(h)], en_ref[at, lanes(h)],
                lim_ref[at, lanes(h)].astype(jnp.float32), shifts_ref[at, :],
                *(sums_ref[s, h, pad + row : pad + row + 1, :] for s in range(4)),
                *(node_ref[d, h, joint, :] for d in range(2)),
            ]
            for k, value in enumerate(kept):
                rim_ref[k, to, lanes(h)] = value

    edge_ref[...] = edges_ref[...].T[0 : 2 * RAW * EDGE, :]

    def third_pass(i, _):
        here = at_rows(i)
        wide = lambda ref, *at: Wide(ref[(*at, here, lanes(h))] for h in halves)
        rho, en = wide(rho_ref), wide(en_ref)
        sx, sy = wide(vel_ref, 0), wide(vel_ref, 1)
        z = Wide(press_ref[0, h, here, :] for h in halves)
        p = Wide(press_ref[1, h, here, :] for h in halves)
        lower = [Wide(node_ref[d, h, here, :] for h in halves) for d in range(2)]
        upper = [Wide(node_ref[d, h, at_rows(i, 1), :] for h in halves) for d in range(2)]
        shift = shifts_ref[here, :]
        cells = wide_cells(z, p, sx, sy, rho, en, lower, upper, right)
        for h, (conserved, scale, ends_left, ends_right) in enumerate(cells):
            for k, value in enumerate((*conserved[1:], scale, *next_weights(shift, ends_left, ends_right))):
                kept_ref[k, h, here, :] = value
        return 0

    def fourth_pass(i, _):
        here = at_rows(i)
        twice = Wide(2.0 * lim_ref[here, lanes(h)].astype(jnp.float32) + 2.0 for h in halves)
        kept = [Wide(kept_ref[k, h, here, :] for h in halves) for k in range(6)]
        rho = Wide(rho_ref[here, lanes(h)] for h in halves)
        for f, conserved in enumerate((rho, *kept[:3])):
            done = wide_field(conserved, kept[3], twice, kept[4:], left, right)
            spot = pl.ds(pl.multiple_of(f * rows + i * STEP, STEP), STEP)
            ends = done.parts[0], done.parts[-1]
            first_ref[spot, :] = jnp.where(even_x, ends[1], ends[0])
            second_ref[spot, :] = jnp.where(even_x, ends[0], ends[1])
        return 0

    lax.fori_loop(0, rows // STEP, third_pass, 0, unroll=BLOCK[2])
    lax.fori_loop(0, rows // STEP, fourth_pass, 0, unroll=BLOCK[3])


def rim_kernel(near_ref, far_ref, kept_ref, edge_ref, first_ref, second_ref, corner_ref):
    cols = near_ref.shape[-1]
    halves = range(cols // TILE)
    even_x = lax.axis_index("gx") % 2 == 0
    level, levels = lax.axis_index("gy"), lax.axis_size("gy")
    even_y = level % 2 == 0
    near, far = near_ref[0:4, :], far_ref[0:4, :]
    below = jnp.where(level == 0, 0.0, jnp.where(even_y, far, near))
    above = jnp.where(level == levels - 1, 0.0, jnp.where(even_y, near, far))

    lane = lax.broadcasted_iota(jnp.int32, (8, TILE), 1)
    bottom = lax.broadcasted_iota(jnp.int32, (8, TILE), 0) == 0
    left = lambda a: Wide(wide_left(lane, a.parts))
    right = lambda a: Wide(wide_right(lane, a.parts))

    kept = [Wide(kept_ref[k, :, lanes(h)] for h in halves) for k in range(14)]
    z, p, sx, sy, rho, en, lim, shift = kept[:8]
    own, joint = kept[8:12], kept[12:14]
    outer = [
        Wide(jnp.where(bottom, cut(below[k : k + 1, :], h), cut(above[k : k + 1, :], h)) for h in halves)
        for k in range(4)
    ]
    outer = column_sums(*outer, left)
    under, over = [], []
    for a, b in zip(outer, own):
        under.append(Wide(jnp.where(bottom, x, y) for x, y in zip(a.parts, b.parts)))
        over.append(Wide(jnp.where(bottom, y, x) for x, y in zip(a.parts, b.parts)))
    fresh = [nodes([q.parts[h] for q in under], [q.parts[h] for q in over]) for h in halves]
    fresh = [Wide(q) for q in zip(*fresh)]
    lower = [Wide(jnp.where(bottom, x, y) for x, y in zip(a.parts, b.parts)) for a, b in zip(fresh, joint)]
    upper = [Wide(jnp.where(bottom, y, x) for x, y in zip(a.parts, b.parts)) for a, b in zip(fresh, joint)]
    cells = wide_cells(z, p, sx, sy, rho, en, lower, upper, right)
    weights = [next_weights(shift.parts[h], *cells[h][2:]) for h in halves]
    weights = [Wide(w) for w in zip(*weights)]
    twice = Wide(2.0 * q + 2.0 for q in lim.parts)
    scale = Wide(c[1] for c in cells)
    for f in range(4):
        conserved = Wide(c[0][f] for c in cells)
        done = wide_field(conserved, scale, twice, weights, left, right)
        ends = done.parts[0][0:2, :], done.parts[-1][0:2, :]
        first_ref[2 * f : 2 * f + 2, :] = jnp.where(even_x, ends[1], ends[0])
        second_ref[2 * f : 2 * f + 2, :] = jnp.where(even_x, ends[0], ends[1])

    halo = jnp.concatenate([below, above], axis=0)
    corner = pltpu.roll(jnp.where(lane < TILE // 2, cut(halo, 0), cut(halo, len(halves) - 1)), EDGE, 1)
    corner = jnp.concatenate([corner, jnp.zeros((TILE - 8, TILE), jnp.float32)], axis=0)
    corner_t = corner.T[0 : 2 * EDGE, :]
    corner_ref[...] = corner_t
    for k in range(RAW + 1):
        at = 2 * k * EDGE
        if k < RAW:
            right_edge, left_edge = edge_ref[at : at + EDGE, :], edge_ref[at + EDGE : at + 2 * EDGE, :]
        else:
            right_edge, left_edge = corner_t[0:EDGE, :], corner_t[EDGE:, :]
        spot = slice(8 + k * EDGE, 8 + (k + 1) * EDGE)
        first_ref[spot, :] = jnp.where(even_x, right_edge, left_edge)
        second_ref[spot, :] = jnp.where(even_x, left_edge, right_edge)


def edge_kernel(edge_ref, corner_ref, from_near_ref, from_far_ref, row_ref, patch_ref):
    rows = patch_ref.shape[0]
    even_x = lax.axis_index("gx") % 2 == 0
    span = 4 * EDGE

    def window(k):
        spot = slice(8 + k * EDGE, 8 + (k + 1) * EDGE)
        own, at = (edge_ref, 2 * k * EDGE) if k < RAW else (corner_ref, 0)
        return jnp.concatenate(
            [
                jnp.where(even_x, from_far_ref[spot, :], from_near_ref[spot, :]),
                own[at + EDGE : at + 2 * EDGE, :],
                own[at : at + EDGE, :],
                jnp.where(even_x, from_near_ref[spot, :], from_far_ref[spot, :]),
            ],
            axis=0,
        )

    left = lambda a: pltpu.roll(a, 1, 0)
    right = lambda a: pltpu.roll(a, span - 1, 0)
    rho, sx, sy, en, mat, lim = (window(k) for k in range(RAW))
    halo = window(RAW)
    z, p = acoustic(rho, en, mat)
    own = column_sums(z, p, sx, sy, left)
    spread = lambda k: jnp.broadcast_to(halo[:, k : k + 1], (span, rows))
    below = column_sums(*(spread(k) for k in range(4)), left)
    above = column_sums(*(spread(k) for k in range(4, 8)), left)
    lane = lax.broadcasted_iota(jnp.int32, (span, rows), 1)
    under = [jnp.where(lane == 0, b, pltpu.roll(a, 1, 1)) for a, b in zip(own, below)]
    over = [jnp.where(lane == rows - 1, b, pltpu.roll(a, rows - 1, 1)) for a, b in zip(own, above)]
    conserved, scale, ends_left, ends_right = cell_update(
        z, p, sx, sy, rho, en, nodes(under, own), nodes(own, over), right
    )
    weights = next_weights(row_ref[0:1, :], ends_left, ends_right)
    fields = [remapped_field(q, scale, 2.0 * lim + 2.0, weights, left, right) for q in conserved]
    patch_ref[...] = jnp.concatenate(fields, axis=0).T


def merge_kernel(
    first_ref, second_ref, from_near_ref, from_far_ref,
    rim_first_ref, rim_second_ref, rim_near_ref, rim_far_ref, patch_ref,
    row_ref, out_hbm, out_ref, sems,
):
    rows = out_ref.shape[1]
    span = 4 * EDGE
    chunks, inner = rows // CHUNK, CHUNK // STEP
    even_x = lax.axis_index("gx") % 2 == 0
    to_left, to_right = row_ref[1:2, :], row_ref[2:3, :]

    def put(here, row, patch, pick):
        goes_left, goes_right = row < to_left, row >= rows - to_right
        lane = lax.broadcasted_iota(jnp.int32, patch.shape, 1)
        head, tail = lane < 3, lane >= TILE - 2
        for f in range(4):
            at_left = pltpu.roll(patch, (-(span * f + EDGE)) % TILE, 1)
            at_right = pltpu.roll(patch, (-(span * f + 3 * EDGE)) % TILE, 1)
            first, second, near, far = pick(f)
            own_0 = jnp.where(head, at_left, jnp.where(even_x, second, first))
            own_1 = jnp.where(tail, at_right, jnp.where(even_x, first, second))
            before = jnp.where(tail, at_left, jnp.where(even_x, far, near))
            after = jnp.where(head, at_right, jnp.where(even_x, near, far))
            out_ref[f, here, lanes(0)] = jnp.where(
                goes_right, before, jnp.where(goes_left, own_1, own_0)
            )
            out_ref[f, here, lanes(1)] = jnp.where(
                goes_right, own_0, jnp.where(goes_left, after, own_1)
            )

    row_in = lax.broadcasted_iota(jnp.int32, (STEP, TILE), 0)

    whole = (first_ref, second_ref, from_near_ref, from_far_ref)
    rims = (rim_first_ref, rim_second_ref, rim_near_ref, rim_far_ref)

    def one(i):
        here = pl.ds(pl.multiple_of(i * STEP, STEP), STEP)

        def pick(f):
            spot = pl.ds(pl.multiple_of(f * rows + i * STEP, STEP), STEP)
            return [ref[spot, :] for ref in whole]

        put(here, (row_in + i * STEP).astype(jnp.float32), patch_ref[here, :], pick)
        return 0

    def rim(r):
        row = r * (rows - 1)
        here = slice(row, row + 1)
        pick = lambda f: [ref[2 * f + r : 2 * f + r + 1, :] for ref in rims]
        put(here, jnp.full((1, TILE), float(row)), patch_ref[here, :], pick)

    def copy(c):
        part = pl.ds(pl.multiple_of(c * CHUNK, CHUNK), CHUNK)
        return pltpu.make_async_copy(out_ref.at[:, part, :], out_hbm.at[:, 0, part, :], sems.at[c])

    def chunk(c, _):
        lax.fori_loop(0, inner, lambda j, _: one(c * inner + j), 0, unroll=MERGE)
        pl.when(c == 0)(lambda: rim(0))
        pl.when(c == chunks - 1)(lambda: rim(1))
        copy(c).start()
        return 0

    lax.fori_loop(0, chunks, chunk, 0)
    for c in range(chunks):
        copy(c).wait()


def on_device(density, velocity, energy, material, limiter, owners, dest_tile, tile_shift):
    planes, rows, cols = density.shape
    assert planes == 1 and rows == TILE and cols == 2 * TILE
    gx, gy = lax.axis_size("gx"), lax.axis_size("gy")
    f32 = jnp.float32
    vmem = pl.BlockSpec(memory_space=pltpu.VMEM)
    hbm = pl.BlockSpec(memory_space=pltpu.HBM)
    shape = lambda *dims: jax.ShapeDtypeStruct(dims, f32)
    params = pltpu.CompilerParams(vmem_limit_bytes=VMEM_LIMIT)
    chunks = rows // CHUNK
    stay = lambda array: pltpu.with_memory_space_constraint(array, pltpu.HBM)

    tile = shape(4 * rows, TILE)
    first, second, edge, kept, near, far, per_row = pl.pallas_call(
        block_kernel,
        in_specs=[hbm] * 7,
        out_specs=[vmem] * 7,
        out_shape=[
            tile,
            tile,
            shape(2 * RAW * EDGE, TILE),
            shape(14, 8, cols),
            shape(8, cols),
            shape(8, cols),
            shape(8, TILE),
        ],
        scratch_shapes=[
            pltpu.VMEM((rows, cols), f32),
            pltpu.VMEM((2, rows, cols), f32),
            pltpu.VMEM((rows, cols), f32),
            pltpu.VMEM((rows, cols), jnp.int32),
            pltpu.VMEM((rows, cols), jnp.int32),
            pltpu.VMEM((1, rows), f32),
            pltpu.VMEM((rows * cols // TILE // TILE, TILE), jnp.int32),
            pltpu.VMEM((4, 2, rows + 16, TILE), f32),
            pltpu.VMEM((2, 2, rows + 8, TILE), f32),
            pltpu.VMEM((2, 2, rows, TILE), f32),
            pltpu.VMEM((TILE, TILE), f32),
            pltpu.VMEM((rows, TILE), f32),
            pltpu.VMEM((6, 2, rows, TILE), f32),
            pltpu.SemaphoreType.DMA((5, chunks)),
            pltpu.SemaphoreType.DMA((2,)),
        ],
        compiler_params=params,
        name="block",
    )(*map(stay, (density, velocity, energy, material, limiter, tile_shift, owners.reshape(-1, TILE))))
    from_near = lax.ppermute(first, "gx", near_pairs(gx))
    from_far = lax.ppermute(second, "gx", far_pairs(gx))
    near = lax.ppermute(near, "gy", near_pairs(gy))
    far = lax.ppermute(far, "gy", far_pairs(gy))

    small = shape(8 + (RAW + 1) * EDGE, TILE)
    small_first, small_second, corner = pl.pallas_call(
        rim_kernel,
        in_specs=[vmem] * 4,
        out_specs=[vmem] * 3,
        out_shape=[small, small, shape(2 * EDGE, TILE)],
        compiler_params=params,
        name="rim",
    )(near, far, kept, edge)
    small_near = lax.ppermute(small_first, "gx", near_pairs(gx))
    small_far = lax.ppermute(small_second, "gx", far_pairs(gx))

    patch = pl.pallas_call(
        edge_kernel,
        in_specs=[vmem] * 5,
        out_specs=vmem,
        out_shape=shape(rows, TILE),
        compiler_params=params,
        name="edge",
    )(edge, corner, small_near, small_far, per_row)

    return pl.pallas_call(
        merge_kernel,
        in_specs=[vmem] * 10,
        out_specs=hbm,
        out_shape=shape(4, planes, rows, cols),
        scratch_shapes=[pltpu.VMEM((4, rows, cols), f32), pltpu.SemaphoreType.DMA((chunks,))],
        compiler_params=params,
        name="merge",
    )(
        first, second, from_near, from_far,
        small_first, small_second, small_near, small_far, patch, per_row,
    )


def solution(mesh):
    assert mesh.shape["gx"] % 2 == 0 and mesh.shape["gy"] % 2 == 0
    placed = (
        P(None, "gy", "gx"),
        P(None, None, "gy", "gx"),
        P(None, "gy", "gx"),
        P(None, "gy", "gx"),
        P(None, "gy", "gx"),
        P(("gx", "gy")),
        P(("gx", "gy")),
        P(None, "gy"),
    )
    return jax.shard_map(
        on_device, mesh=mesh, in_specs=placed, out_specs=P(None, None, "gy", "gx"), check_vma=False
    )
```

```python
import jax
import jax.numpy as jnp
from jax import lax
from jax.experimental import pallas as pl
from jax.experimental.pallas import tpu as pltpu
from jax.sharding import PartitionSpec as P


TILE = 128
time_step = 0.05
STEP = 8
BLOCK = (8, 8, 16, 8)
MERGE = 8
EDGES = 4
LOAD = 64
CHUNK = 64
VMEM_LIMIT = 8 << 20
EDGE = 8
RAW = 6


def near_pairs(count):
    return [(i, i ^ 1) for i in range(count)]


def far_pairs(count):
    pairs = []
    for i in range(1, count, 2):
        pairs += [(i, (i + 1) % count), ((i + 1) % count, i)]
    return pairs


def acoustic(density, energy, material):
    first, second = material == 0, material == 1
    less_one = jnp.where(first, 0.4, jnp.where(second, 2.0 / 3.0, 2.0)).astype(jnp.float32)
    both = jnp.where(first, 1.4 * 0.4, jnp.where(second, 10.0 / 9.0, 6.0)).astype(jnp.float32)
    return density * jnp.sqrt(both * energy), less_one * density * energy


def column_sums(impedance, pressure, speed_x, speed_y, from_left):
    along_x, along_y = impedance * speed_x, impedance * speed_y
    up, down = along_y + pressure, along_y - pressure
    return (
        from_left(impedance) + impedance,
        from_left(along_x + pressure) + (along_x - pressure),
        from_left(up) + up,
        from_left(down) + down,
    )


def nodes(below, above):
    scale = 1.0 / (below[0] + above[0])
    return (below[1] + above[1]) * scale, (below[2] + above[3]) * scale


def cell_update(impedance, pressure, speed_x, speed_y, density, energy, lower, upper, from_right):
    side_x = lower[0] + upper[0]
    side_y = lower[1] + upper[1]
    rise_y = upper[1] - lower[1]
    square = lower[0] * lower[0] + upper[0] * upper[0] + lower[1] * lower[1] + upper[1] * upper[1]
    far_x = from_right(side_x)
    sum_x = side_x + far_x
    sum_y = side_y + from_right(side_y)
    half_z = (0.5 * time_step) * impedance
    volume = (far_x - side_x) + (rise_y + from_right(rise_y))
    relaxation = (square + from_right(square)) - speed_x * sum_x - speed_y * sum_y
    left = (0.5 * time_step) * side_x
    right = (0.5 * time_step) * far_x
    total = density * (energy + 0.5 * (speed_x * speed_x + speed_y * speed_y))
    conserved = (
        density,
        density * speed_x + half_z * (sum_x - 4.0 * speed_x),
        density * speed_y + half_z * (sum_y - 4.0 * speed_y),
        total + (half_z * relaxation - (0.5 * time_step) * pressure * volume),
    )
    return conserved, 0.5 / (1.0 + (right - left)), left, right


def next_weights(shift, left, right):
    start = shift + left
    stop = (1.0 + shift) + right
    low = jnp.maximum(start, 1.0)
    span = jnp.maximum(stop - low, 0.0)
    return 2.0 * span, (0.5 * span) * (low - start)


def limited(back, fore, twice):
    low = jnp.minimum(twice * jnp.maximum(back, fore), 0.0)
    high = jnp.maximum(twice * jnp.minimum(back, fore), 0.0)
    return jnp.minimum(jnp.maximum(back + fore, low), high)


def remapped_field(conserved, scale, twice, weights, from_left, from_right):
    half = conserved * scale
    back = half - from_left(half)
    slope = limited(back, from_right(back), twice)
    onward = weights[0] * half + weights[1] * slope
    return (conserved - onward) + from_left(onward)


class Wide:
    def __init__(self, parts):
        self.parts = tuple(parts)

    def _with(self, other, op):
        if isinstance(other, Wide):
            return Wide(op(a, b) for a, b in zip(self.parts, other.parts))
        return Wide(op(a, other) for a in self.parts)

    def __add__(self, o):
        return self._with(o, lambda a, b: a + b)

    def __radd__(self, o):
        return self._with(o, lambda a, b: b + a)

    def __sub__(self, o):
        return self._with(o, lambda a, b: a - b)

    def __mul__(self, o):
        return self._with(o, lambda a, b: a * b)

    def __rmul__(self, o):
        return self._with(o, lambda a, b: b * a)


def wide_left(lane, parts):
    turned = [pltpu.roll(a, 1, 1) for a in parts]
    return [turned[0]] + [
        jnp.where(lane == 0, turned[i - 1], turned[i]) for i in range(1, len(turned))
    ]


def wide_right(lane, parts):
    width = parts[0].shape[-1]
    turned = [pltpu.roll(a, width - 1, 1) for a in parts]
    return [
        jnp.where(lane == width - 1, turned[i + 1], turned[i]) for i in range(len(turned) - 1)
    ] + [turned[-1]]


def cut(array, h):
    return array[:, h * TILE : (h + 1) * TILE]


def lanes(h):
    return slice(h * TILE, (h + 1) * TILE)


def wide_cells(z, p, sx, sy, rho, en, lower, upper, from_right):
    parts = range(len(z.parts))
    pieces = []
    for h in parts:
        lx, ly, ux, uy = (q.parts[h] for q in (*lower, *upper))
        pieces.append((lx + ux, ly + uy, uy - ly, lx * lx + ux * ux + ly * ly + uy * uy))
    far = [from_right(Wide(q)).parts for q in zip(*pieces)]
    results = []
    for h in parts:
        order = iter([far[k][h] for k in range(4)])
        results.append(
            cell_update(
                z.parts[h], p.parts[h], sx.parts[h], sy.parts[h], rho.parts[h], en.parts[h],
                [q.parts[h] for q in lower], [q.parts[h] for q in upper], lambda _: next(order),
            )
        )
    return results


def wide_field(conserved, scale, twice, weights, left, right):
    half = conserved * scale
    back = half - left(half)
    fore = right(back)
    onward = []
    for h in range(len(half.parts)):
        slope = limited(back.parts[h], fore.parts[h], twice.parts[h])
        onward.append(weights[0].parts[h] * half.parts[h] + weights[1].parts[h] * slope)
    onward = Wide(onward)
    return (conserved - onward) + left(onward)


def block_kernel(
    rho_hbm, vel_hbm, en_hbm, mat_hbm, lim_hbm, shift_hbm, owner_hbm,
    first_ref, second_ref, near_ref, far_ref, rho_ref, vel_ref, en_ref, mat_ref, lim_ref, owner_ref,
    sums_ref, node_ref, press_ref, shifts_ref, shift_ref, kept_ref, sems, small_sems,
):
    rows, cols = rho_ref.shape
    halves = range(cols // TILE)
    even_x = lax.axis_index("gx") % 2 == 0
    even_y = lax.axis_index("gy") % 2 == 0
    pad = 8
    chunks, inner = rows // LOAD, LOAD // STEP

    def copies(c):
        part = pl.ds(pl.multiple_of(c * LOAD, LOAD), LOAD)
        return [
            pltpu.make_async_copy(rho_hbm.at[0, part, :], rho_ref.at[part, :], sems.at[0, c]),
            pltpu.make_async_copy(en_hbm.at[0, part, :], en_ref.at[part, :], sems.at[1, c]),
            pltpu.make_async_copy(mat_hbm.at[0, part, :], mat_ref.at[part, :], sems.at[2, c]),
            pltpu.make_async_copy(vel_hbm.at[:, 0, part, :], vel_ref.at[:, part, :], sems.at[3, c]),
            pltpu.make_async_copy(lim_hbm.at[0, part, :], lim_ref.at[part, :], sems.at[4, c]),
        ]

    for c in range(chunks):
        for copy in copies(c):
            copy.start()

    small = [
        pltpu.make_async_copy(shift_hbm, shift_ref, small_sems.at[0]),
        pltpu.make_async_copy(owner_hbm, owner_ref, small_sems.at[1]),
    ]
    for copy in small:
        copy.start()
    lane = lax.broadcasted_iota(jnp.int32, (STEP, TILE), 1)
    left = lambda a: Wide(wide_left(lane, a.parts))
    right = lambda a: Wide(wide_right(lane, a.parts))

    def at_rows(i, offset=0):
        return pl.ds(pl.multiple_of(i * STEP, STEP) + offset, STEP)

    def first_pass(i):
        here = at_rows(i)
        rho = [rho_ref[here, lanes(h)] for h in halves]
        en = [en_ref[here, lanes(h)] for h in halves]
        mat = [mat_ref[here, lanes(h)] for h in halves]
        sx = [vel_ref[0, here, lanes(h)] for h in halves]
        sy = [vel_ref[1, here, lanes(h)] for h in halves]
        both = [acoustic(rho[h], en[h], mat[h]) for h in halves]
        z, p = [b[0] for b in both], [b[1] for b in both]
        for h in halves:
            press_ref[0, h, here, :] = z[h]
            press_ref[1, h, here, :] = p[h]
        totals = column_sums(Wide(z), Wide(p), Wide(sx), Wide(sy), left)
        for s, total in enumerate(totals):
            for h in halves:
                sums_ref[s, h, at_rows(i, pad), :] = total.parts[h]
        return 0

    def first_chunk(c, _):
        for copy in copies(c):
            copy.wait()
        step = lambda j, _: first_pass(c * inner + j)
        return lax.fori_loop(0, inner, step, 0, unroll=BLOCK[0])

    for s in range(4):
        for h in halves:
            sums_ref[s, h, 0:pad, :] = jnp.full((pad, TILE), float(s == 0), jnp.float32)
            sums_ref[s, h, rows + pad :, :] = jnp.full((pad, TILE), float(s == 0), jnp.float32)
    lax.fori_loop(0, chunks, first_chunk, 0)

    def second_pass(i, _):
        for h in halves:
            under = [sums_ref[s, h, at_rows(i, pad - 1), :] for s in range(3)]
            over = [sums_ref[s, h, at_rows(i, pad), :] for s in (0, 1, 3)]
            nx, ny = nodes(under, [over[0], over[1], None, over[2]])
            node_ref[0, h, at_rows(i), :] = nx
            node_ref[1, h, at_rows(i), :] = ny
        return 0

    for copy in small:
        copy.wait()
    shifts_ref[...] = jnp.broadcast_to(shift_ref[...], (TILE, TILE)).T
    lax.fori_loop(0, rows // STEP, second_pass, 0, unroll=BLOCK[1])
    for h in halves:
        for d in range(2):
            node_ref[d, h, rows : rows + STEP, :] = jnp.zeros((STEP, TILE), jnp.float32)

    for k in range(4):
        for h in halves:
            pick = lambda row: (
                press_ref[k, h, row : row + 1, :]
                if k < 2
                else vel_ref[k - 2, row : row + 1, lanes(h)]
            )
            top, bottom = pick(rows - 1), pick(0)
            near_ref[k : k + 1, lanes(h)] = jnp.where(even_y, top, bottom)
            far_ref[k : k + 1, lanes(h)] = jnp.where(even_y, bottom, top)

    def third_pass(i, _):
        here = at_rows(i)
        wide = lambda ref, *at: Wide(ref[(*at, here, lanes(h))] for h in halves)
        rho, en = wide(rho_ref), wide(en_ref)
        sx, sy = wide(vel_ref, 0), wide(vel_ref, 1)
        z = Wide(press_ref[0, h, here, :] for h in halves)
        p = Wide(press_ref[1, h, here, :] for h in halves)
        lower = [Wide(node_ref[d, h, here, :] for h in halves) for d in range(2)]
        upper = [Wide(node_ref[d, h, at_rows(i, 1), :] for h in halves) for d in range(2)]
        shift = shifts_ref[here, :]
        cells = wide_cells(z, p, sx, sy, rho, en, lower, upper, right)
        for h, (conserved, scale, ends_left, ends_right) in enumerate(cells):
            for k, value in enumerate((*conserved[1:], scale, *next_weights(shift, ends_left, ends_right))):
                kept_ref[k, h, here, :] = value
        return 0

    def fourth_pass(i, _):
        here = at_rows(i)
        twice = Wide(2.0 * lim_ref[here, lanes(h)].astype(jnp.float32) + 2.0 for h in halves)
        kept = [Wide(kept_ref[k, h, here, :] for h in halves) for k in range(6)]
        rho = Wide(rho_ref[here, lanes(h)] for h in halves)
        for f, conserved in enumerate((rho, *kept[:3])):
            done = wide_field(conserved, kept[3], twice, kept[4:], left, right)
            spot = pl.ds(pl.multiple_of(f * rows + i * STEP, STEP), STEP)
            ends = done.parts[0], done.parts[-1]
            first_ref[spot, :] = jnp.where(even_x, ends[1], ends[0])
            second_ref[spot, :] = jnp.where(even_x, ends[0], ends[1])
        return 0

    lax.fori_loop(0, rows // STEP, third_pass, 0, unroll=BLOCK[2])
    lax.fori_loop(0, rows // STEP, fourth_pass, 0, unroll=BLOCK[3])


def rows_kernel(
    rho_ref, vel_ref, en_ref, mat_ref, lim_ref, owner_ref, sums_ref, node_ref, press_ref, shifts_ref,
    edge_ref, rim_ref, row_ref, edges_ref,
):
    rows, cols = rho_ref.shape
    halves = range(cols // TILE)
    pad = 8
    lane = lax.broadcasted_iota(jnp.int32, (STEP, TILE), 1)

    def edges(i, _):
        here = pl.ds(pl.multiple_of(i * STEP, STEP), STEP)
        edge = jnp.zeros((STEP, TILE), jnp.float32)
        ends = [
            [ref[(*at, here, lanes(h))].astype(jnp.float32) for h in (0, len(halves) - 1)]
            for ref, *at in ((rho_ref,), (vel_ref, 0), (vel_ref, 1), (en_ref,), (mat_ref,), (lim_ref,))
        ]
        for k, (start, stop) in enumerate(ends):
            turned = pltpu.roll(jnp.where(lane < TILE // 2, start, stop), (2 * k + 1) * EDGE, 1)
            edge = jnp.where(lane >= 2 * k * EDGE, turned, edge)
        edges_ref[here, :] = edge
        return 0

    lax.fori_loop(0, rows // STEP, edges, 0, unroll=EDGES)
    row_ref[0:1, :] = shifts_ref[...].T[0:1, :]
    column, count = lax.axis_index("gx"), lax.axis_size("gx")
    owner = owner_ref[...]
    for k, which in enumerate(((column + count - 1) % count, (column + 1) % count)):
        hits = jnp.where(owner == which, 1.0, 0.0)
        total = jnp.sum(jnp.sum(hits, axis=1, keepdims=True), axis=0, keepdims=True)
        row_ref[k + 1 : k + 2, :] = jnp.broadcast_to(total, (1, TILE))
    for r, row in enumerate((0, rows - 1)):
        at, to = slice(row, row + 1), slice(r, r + 1)
        joint = slice(1, 2) if r == 0 else slice(rows - 1, rows)
        for h in halves:
            kept = [
                press_ref[0, h, at, :], press_ref[1, h, at, :],
                vel_ref[0, at, lanes(h)], vel_ref[1, at, lanes(h)],
                rho_ref[at, lanes(h)], en_ref[at, lanes(h)],
                lim_ref[at, lanes(h)].astype(jnp.float32), shifts_ref[at, :],
                *(sums_ref[s, h, pad + row : pad + row + 1, :] for s in range(4)),
                *(node_ref[d, h, joint, :] for d in range(2)),
            ]
            for k, value in enumerate(kept):
                rim_ref[k, to, lanes(h)] = value

    edge_ref[...] = edges_ref[...].T[0 : 2 * RAW * EDGE, :]


def rim_kernel(near_ref, far_ref, kept_ref, edge_ref, first_ref, second_ref, corner_ref):
    cols = near_ref.shape[-1]
    halves = range(cols // TILE)
    even_x = lax.axis_index("gx") % 2 == 0
    level, levels = lax.axis_index("gy"), lax.axis_size("gy")
    even_y = level % 2 == 0
    near, far = near_ref[0:4, :], far_ref[0:4, :]
    below = jnp.where(level == 0, 0.0, jnp.where(even_y, far, near))
    above = jnp.where(level == levels - 1, 0.0, jnp.where(even_y, near, far))

    lane = lax.broadcasted_iota(jnp.int32, (8, TILE), 1)
    bottom = lax.broadcasted_iota(jnp.int32, (8, TILE), 0) == 0
    left = lambda a: Wide(wide_left(lane, a.parts))
    right = lambda a: Wide(wide_right(lane, a.parts))

    kept = [Wide(kept_ref[k, :, lanes(h)] for h in halves) for k in range(14)]
    z, p, sx, sy, rho, en, lim, shift = kept[:8]
    own, joint = kept[8:12], kept[12:14]
    outer = [
        Wide(jnp.where(bottom, cut(below[k : k + 1, :], h), cut(above[k : k + 1, :], h)) for h in halves)
        for k in range(4)
    ]
    outer = column_sums(*outer, left)
    under, over = [], []
    for a, b in zip(outer, own):
        under.append(Wide(jnp.where(bottom, x, y) for x, y in zip(a.parts, b.parts)))
        over.append(Wide(jnp.where(bottom, y, x) for x, y in zip(a.parts, b.parts)))
    fresh = [nodes([q.parts[h] for q in under], [q.parts[h] for q in over]) for h in halves]
    fresh = [Wide(q) for q in zip(*fresh)]
    lower = [Wide(jnp.where(bottom, x, y) for x, y in zip(a.parts, b.parts)) for a, b in zip(fresh, joint)]
    upper = [Wide(jnp.where(bottom, y, x) for x, y in zip(a.parts, b.parts)) for a, b in zip(fresh, joint)]
    cells = wide_cells(z, p, sx, sy, rho, en, lower, upper, right)
    weights = [next_weights(shift.parts[h], *cells[h][2:]) for h in halves]
    weights = [Wide(w) for w in zip(*weights)]
    twice = Wide(2.0 * q + 2.0 for q in lim.parts)
    scale = Wide(c[1] for c in cells)
    for f in range(4):
        conserved = Wide(c[0][f] for c in cells)
        done = wide_field(conserved, scale, twice, weights, left, right)
        ends = done.parts[0][0:2, :], done.parts[-1][0:2, :]
        first_ref[2 * f : 2 * f + 2, :] = jnp.where(even_x, ends[1], ends[0])
        second_ref[2 * f : 2 * f + 2, :] = jnp.where(even_x, ends[0], ends[1])

    halo = jnp.concatenate([below, above], axis=0)
    corner = pltpu.roll(jnp.where(lane < TILE // 2, cut(halo, 0), cut(halo, len(halves) - 1)), EDGE, 1)
    corner = jnp.concatenate([corner, jnp.zeros((TILE - 8, TILE), jnp.float32)], axis=0)
    corner_t = corner.T[0 : 2 * EDGE, :]
    corner_ref[...] = corner_t
    for k in range(RAW + 1):
        at = 2 * k * EDGE
        if k < RAW:
            right_edge, left_edge = edge_ref[at : at + EDGE, :], edge_ref[at + EDGE : at + 2 * EDGE, :]
        else:
            right_edge, left_edge = corner_t[0:EDGE, :], corner_t[EDGE:, :]
        spot = slice(8 + k * EDGE, 8 + (k + 1) * EDGE)
        first_ref[spot, :] = jnp.where(even_x, right_edge, left_edge)
        second_ref[spot, :] = jnp.where(even_x, left_edge, right_edge)


def edge_kernel(edge_ref, corner_ref, from_near_ref, from_far_ref, row_ref, patch_ref):
    rows = patch_ref.shape[0]
    even_x = lax.axis_index("gx") % 2 == 0
    span = 4 * EDGE

    def window(k):
        spot = slice(8 + k * EDGE, 8 + (k + 1) * EDGE)
        own, at = (edge_ref, 2 * k * EDGE) if k < RAW else (corner_ref, 0)
        return jnp.concatenate(
            [
                jnp.where(even_x, from_far_ref[spot, :], from_near_ref[spot, :]),
                own[at + EDGE : at + 2 * EDGE, :],
                own[at : at + EDGE, :],
                jnp.where(even_x, from_near_ref[spot, :], from_far_ref[spot, :]),
            ],
            axis=0,
        )

    left = lambda a: pltpu.roll(a, 1, 0)
    right = lambda a: pltpu.roll(a, span - 1, 0)
    rho, sx, sy, en, mat, lim = (window(k) for k in range(RAW))
    halo = window(RAW)
    z, p = acoustic(rho, en, mat)
    own = column_sums(z, p, sx, sy, left)
    spread = lambda k: jnp.broadcast_to(halo[:, k : k + 1], (span, rows))
    below = column_sums(*(spread(k) for k in range(4)), left)
    above = column_sums(*(spread(k) for k in range(4, 8)), left)
    lane = lax.broadcasted_iota(jnp.int32, (span, rows), 1)
    under = [jnp.where(lane == 0, b, pltpu.roll(a, 1, 1)) for a, b in zip(own, below)]
    over = [jnp.where(lane == rows - 1, b, pltpu.roll(a, rows - 1, 1)) for a, b in zip(own, above)]
    conserved, scale, ends_left, ends_right = cell_update(
        z, p, sx, sy, rho, en, nodes(under, own), nodes(own, over), right
    )
    weights = next_weights(row_ref[0:1, :], ends_left, ends_right)
    fields = [remapped_field(q, scale, 2.0 * lim + 2.0, weights, left, right) for q in conserved]
    patch_ref[...] = jnp.concatenate(fields, axis=0).T


def merge_kernel(
    first_ref, second_ref, from_near_ref, from_far_ref,
    rim_first_ref, rim_second_ref, rim_near_ref, rim_far_ref, patch_ref,
    row_ref, out_hbm, out_ref, sems,
):
    rows = out_ref.shape[1]
    span = 4 * EDGE
    chunks, inner = rows // CHUNK, CHUNK // STEP
    even_x = lax.axis_index("gx") % 2 == 0
    to_left, to_right = row_ref[1:2, :], row_ref[2:3, :]

    def put(here, row, patch, pick):
        goes_left, goes_right = row < to_left, row >= rows - to_right
        lane = lax.broadcasted_iota(jnp.int32, patch.shape, 1)
        head, tail = lane < 3, lane >= TILE - 2
        for f in range(4):
            at_left = pltpu.roll(patch, (-(span * f + EDGE)) % TILE, 1)
            at_right = pltpu.roll(patch, (-(span * f + 3 * EDGE)) % TILE, 1)
            first, second, near, far = pick(f)
            own_0 = jnp.where(head, at_left, jnp.where(even_x, second, first))
            own_1 = jnp.where(tail, at_right, jnp.where(even_x, first, second))
            before = jnp.where(tail, at_left, jnp.where(even_x, far, near))
            after = jnp.where(head, at_right, jnp.where(even_x, near, far))
            out_ref[f, here, lanes(0)] = jnp.where(
                goes_right, before, jnp.where(goes_left, own_1, own_0)
            )
            out_ref[f, here, lanes(1)] = jnp.where(
                goes_right, own_0, jnp.where(goes_left, after, own_1)
            )

    row_in = lax.broadcasted_iota(jnp.int32, (STEP, TILE), 0)

    whole = (first_ref, second_ref, from_near_ref, from_far_ref)
    rims = (rim_first_ref, rim_second_ref, rim_near_ref, rim_far_ref)

    def one(i):
        here = pl.ds(pl.multiple_of(i * STEP, STEP), STEP)

        def pick(f):
            spot = pl.ds(pl.multiple_of(f * rows + i * STEP, STEP), STEP)
            return [ref[spot, :] for ref in whole]

        put(here, (row_in + i * STEP).astype(jnp.float32), patch_ref[here, :], pick)
        return 0

    def rim(r):
        row = r * (rows - 1)
        here = slice(row, row + 1)
        pick = lambda f: [ref[2 * f + r : 2 * f + r + 1, :] for ref in rims]
        put(here, jnp.full((1, TILE), float(row)), patch_ref[here, :], pick)

    def copy(c):
        part = pl.ds(pl.multiple_of(c * CHUNK, CHUNK), CHUNK)
        return pltpu.make_async_copy(out_ref.at[:, part, :], out_hbm.at[:, 0, part, :], sems.at[c])

    def chunk(c, _):
        lax.fori_loop(0, inner, lambda j, _: one(c * inner + j), 0, unroll=MERGE)
        pl.when(c == 0)(lambda: rim(0))
        pl.when(c == chunks - 1)(lambda: rim(1))
        copy(c).start()
        return 0

    lax.fori_loop(0, chunks, chunk, 0)
    for c in range(chunks):
        copy(c).wait()


def on_device(density, velocity, energy, material, limiter, owners, dest_tile, tile_shift):
    planes, rows, cols = density.shape
    assert planes == 1 and rows == TILE and cols == 2 * TILE
    gx, gy = lax.axis_size("gx"), lax.axis_size("gy")
    f32 = jnp.float32
    vmem = pl.BlockSpec(memory_space=pltpu.VMEM)
    hbm = pl.BlockSpec(memory_space=pltpu.HBM)
    shape = lambda *dims: jax.ShapeDtypeStruct(dims, f32)
    params = pltpu.CompilerParams(vmem_limit_bytes=VMEM_LIMIT)
    chunks = rows // LOAD
    stay = lambda array: pltpu.with_memory_space_constraint(array, pltpu.HBM)

    tile = shape(4 * rows, TILE)
    i32 = lambda *dims: jax.ShapeDtypeStruct(dims, jnp.int32)
    tile = shape(4 * rows, TILE)
    first, second, near, far, *inner = pl.pallas_call(
        block_kernel,
        in_specs=[hbm] * 7,
        out_specs=[vmem] * 14,
        out_shape=[
            tile,
            tile,
            shape(8, cols),
            shape(8, cols),
            shape(rows, cols),
            shape(2, rows, cols),
            shape(rows, cols),
            i32(rows, cols),
            i32(rows, cols),
            i32(rows * cols // TILE // TILE, TILE),
            shape(4, 2, rows + 16, TILE),
            shape(2, 2, rows + 8, TILE),
            shape(2, 2, rows, TILE),
            shape(rows, TILE),
        ],
        scratch_shapes=[
            pltpu.VMEM((1, rows), f32),
            pltpu.VMEM((6, 2, rows, TILE), f32),
            pltpu.SemaphoreType.DMA((5, chunks)),
            pltpu.SemaphoreType.DMA((2,)),
        ],
        compiler_params=params,
        name="block",
    )(*map(stay, (density, velocity, energy, material, limiter, tile_shift, owners.reshape(-1, TILE))))
    from_near = lax.ppermute(first, "gx", near_pairs(gx))
    from_far = lax.ppermute(second, "gx", far_pairs(gx))
    edge, kept, per_row = pl.pallas_call(
        rows_kernel,
        in_specs=[vmem] * 10,
        out_specs=[vmem] * 3,
        out_shape=[
            shape(2 * RAW * EDGE, TILE),
            shape(14, 8, cols),
            shape(8, TILE),
        ],
        scratch_shapes=[pltpu.VMEM((rows, TILE), f32)],
        compiler_params=params,
        name="outer",
    )(*inner)
    near = lax.ppermute(near, "gy", near_pairs(gy))
    far = lax.ppermute(far, "gy", far_pairs(gy))

    small = shape(8 + (RAW + 1) * EDGE, TILE)
    small_first, small_second, corner = pl.pallas_call(
        rim_kernel,
        in_specs=[vmem] * 4,
        out_specs=[vmem] * 3,
        out_shape=[small, small, shape(2 * EDGE, TILE)],
        compiler_params=params,
        name="rim",
    )(near, far, kept, edge)
    small_near = lax.ppermute(small_first, "gx", near_pairs(gx))
    small_far = lax.ppermute(small_second, "gx", far_pairs(gx))

    patch = pl.pallas_call(
        edge_kernel,
        in_specs=[vmem] * 5,
        out_specs=vmem,
        out_shape=shape(rows, TILE),
        compiler_params=params,
        name="edge",
    )(edge, corner, small_near, small_far, per_row)

    return pl.pallas_call(
        merge_kernel,
        in_specs=[vmem] * 10,
        out_specs=hbm,
        out_shape=shape(4, planes, rows, cols),
        scratch_shapes=[pltpu.VMEM((4, rows, cols), f32), pltpu.SemaphoreType.DMA((rows // CHUNK,))],
        compiler_params=params,
        name="merge",
    )(
        first, second, from_near, from_far,
        small_first, small_second, small_near, small_far, patch, per_row,
    )


def solution(mesh):
    assert mesh.shape["gx"] % 2 == 0 and mesh.shape["gy"] % 2 == 0
    placed = (
        P(None, "gy", "gx"),
        P(None, None, "gy", "gx"),
        P(None, "gy", "gx"),
        P(None, "gy", "gx"),
        P(None, "gy", "gx"),
        P(("gx", "gy")),
        P(("gx", "gy")),
        P(None, "gy"),
    )
    return jax.shard_map(
        on_device, mesh=mesh, in_specs=placed, out_specs=P(None, None, "gy", "gx"), check_vma=False
    )
```

```python
import jax
import jax.numpy as jnp
from jax import lax
from jax.experimental import pallas as pl
from jax.experimental.pallas import tpu as pltpu
from jax.sharding import PartitionSpec as P


TILE = 128
time_step = 0.05
STEP = 8
BLOCK = (8, 8, 16, 8)
MERGE = 8
EDGES = 8
LOAD = 64
CHUNK = 64
VMEM_LIMIT = 8 << 20
EDGE = 5
SPAN = 24
RAW = 6


def near_pairs(count):
    return [(i, i ^ 1) for i in range(count)]


def far_pairs(count):
    pairs = []
    for i in range(1, count, 2):
        pairs += [(i, (i + 1) % count), ((i + 1) % count, i)]
    return pairs


def acoustic(density, energy, material):
    first, second = material == 0, material == 1
    less_one = jnp.where(first, 0.4, jnp.where(second, 2.0 / 3.0, 2.0)).astype(jnp.float32)
    both = jnp.where(first, 1.4 * 0.4, jnp.where(second, 10.0 / 9.0, 6.0)).astype(jnp.float32)
    return density * jnp.sqrt(both * energy), less_one * density * energy


def column_sums(impedance, pressure, speed_x, speed_y, from_left):
    along_x, along_y = impedance * speed_x, impedance * speed_y
    up, down = along_y + pressure, along_y - pressure
    return (
        from_left(impedance) + impedance,
        from_left(along_x + pressure) + (along_x - pressure),
        from_left(up) + up,
        from_left(down) + down,
    )


def nodes(below, above):
    scale = 1.0 / (below[0] + above[0])
    return (below[1] + above[1]) * scale, (below[2] + above[3]) * scale


def cell_update(impedance, pressure, speed_x, speed_y, density, energy, lower, upper, from_right):
    side_x = lower[0] + upper[0]
    side_y = lower[1] + upper[1]
    rise_y = upper[1] - lower[1]
    square = lower[0] * lower[0] + upper[0] * upper[0] + lower[1] * lower[1] + upper[1] * upper[1]
    far_x = from_right(side_x)
    sum_x = side_x + far_x
    sum_y = side_y + from_right(side_y)
    half_z = (0.5 * time_step) * impedance
    volume = (far_x - side_x) + (rise_y + from_right(rise_y))
    relaxation = (square + from_right(square)) - speed_x * sum_x - speed_y * sum_y
    left = (0.5 * time_step) * side_x
    right = (0.5 * time_step) * far_x
    total = density * (energy + 0.5 * (speed_x * speed_x + speed_y * speed_y))
    conserved = (
        density,
        density * speed_x + half_z * (sum_x - 4.0 * speed_x),
        density * speed_y + half_z * (sum_y - 4.0 * speed_y),
        total + (half_z * relaxation - (0.5 * time_step) * pressure * volume),
    )
    return conserved, 0.5 / (1.0 + (right - left)), left, right


def next_weights(shift, left, right):
    start = shift + left
    stop = (1.0 + shift) + right
    low = jnp.maximum(start, 1.0)
    span = jnp.maximum(stop - low, 0.0)
    return 2.0 * span, (0.5 * span) * (low - start)


def limited(back, fore, twice):
    low = jnp.minimum(twice * jnp.maximum(back, fore), 0.0)
    high = jnp.maximum(twice * jnp.minimum(back, fore), 0.0)
    return jnp.minimum(jnp.maximum(back + fore, low), high)


def remapped_field(conserved, scale, twice, weights, from_left, from_right):
    half = conserved * scale
    back = half - from_left(half)
    slope = limited(back, from_right(back), twice)
    onward = weights[0] * half + weights[1] * slope
    return (conserved - onward) + from_left(onward)


class Wide:
    def __init__(self, parts):
        self.parts = tuple(parts)

    def _with(self, other, op):
        if isinstance(other, Wide):
            return Wide(op(a, b) for a, b in zip(self.parts, other.parts))
        return Wide(op(a, other) for a in self.parts)

    def __add__(self, o):
        return self._with(o, lambda a, b: a + b)

    def __radd__(self, o):
        return self._with(o, lambda a, b: b + a)

    def __sub__(self, o):
        return self._with(o, lambda a, b: a - b)

    def __mul__(self, o):
        return self._with(o, lambda a, b: a * b)

    def __rmul__(self, o):
        return self._with(o, lambda a, b: b * a)


def wide_left(lane, parts):
    turned = [pltpu.roll(a, 1, 1) for a in parts]
    return [turned[0]] + [
        jnp.where(lane == 0, turned[i - 1], turned[i]) for i in range(1, len(turned))
    ]


def wide_right(lane, parts):
    width = parts[0].shape[-1]
    turned = [pltpu.roll(a, width - 1, 1) for a in parts]
    return [
        jnp.where(lane == width - 1, turned[i + 1], turned[i]) for i in range(len(turned) - 1)
    ] + [turned[-1]]


def cut(array, h):
    return array[:, h * TILE : (h + 1) * TILE]


def lanes(h):
    return slice(h * TILE, (h + 1) * TILE)


def wide_cells(z, p, sx, sy, rho, en, lower, upper, from_right):
    parts = range(len(z.parts))
    pieces = []
    for h in parts:
        lx, ly, ux, uy = (q.parts[h] for q in (*lower, *upper))
        pieces.append((lx + ux, ly + uy, uy - ly, lx * lx + ux * ux + ly * ly + uy * uy))
    far = [from_right(Wide(q)).parts for q in zip(*pieces)]
    results = []
    for h in parts:
        order = iter([far[k][h] for k in range(4)])
        results.append(
            cell_update(
                z.parts[h], p.parts[h], sx.parts[h], sy.parts[h], rho.parts[h], en.parts[h],
                [q.parts[h] for q in lower], [q.parts[h] for q in upper], lambda _: next(order),
            )
        )
    return results


def wide_field(conserved, scale, twice, weights, left, right):
    half = conserved * scale
    back = half - left(half)
    fore = right(back)
    onward = []
    for h in range(len(half.parts)):
        slope = limited(back.parts[h], fore.parts[h], twice.parts[h])
        onward.append(weights[0].parts[h] * half.parts[h] + weights[1].parts[h] * slope)
    onward = Wide(onward)
    return (conserved - onward) + left(onward)


def block_kernel(
    rho_hbm, vel_hbm, en_hbm, mat_hbm, lim_hbm, shift_hbm, owner_hbm,
    first_ref, second_ref, near_ref, far_ref, rho_ref, vel_ref, en_ref, mat_ref, lim_ref, owner_ref,
    sums_ref, node_ref, press_ref, shifts_ref, shift_ref, kept_ref, sems, small_sems,
):
    rows, cols = rho_ref.shape
    halves = range(cols // TILE)
    even_x = lax.axis_index("gx") % 2 == 0
    even_y = lax.axis_index("gy") % 2 == 0
    pad = 8
    chunks, inner = rows // LOAD, LOAD // STEP

    def copies(c):
        part = pl.ds(pl.multiple_of(c * LOAD, LOAD), LOAD)
        return [
            pltpu.make_async_copy(rho_hbm.at[0, part, :], rho_ref.at[part, :], sems.at[0, c]),
            pltpu.make_async_copy(en_hbm.at[0, part, :], en_ref.at[part, :], sems.at[1, c]),
            pltpu.make_async_copy(mat_hbm.at[0, part, :], mat_ref.at[part, :], sems.at[2, c]),
            pltpu.make_async_copy(vel_hbm.at[:, 0, part, :], vel_ref.at[:, part, :], sems.at[3, c]),
            pltpu.make_async_copy(lim_hbm.at[0, part, :], lim_ref.at[part, :], sems.at[4, c]),
        ]

    for c in range(chunks):
        for copy in copies(c):
            copy.start()

    small = [
        pltpu.make_async_copy(shift_hbm, shift_ref, small_sems.at[0]),
        pltpu.make_async_copy(owner_hbm, owner_ref, small_sems.at[1]),
    ]
    for copy in small:
        copy.start()
    lane = lax.broadcasted_iota(jnp.int32, (STEP, TILE), 1)
    left = lambda a: Wide(wide_left(lane, a.parts))
    right = lambda a: Wide(wide_right(lane, a.parts))

    def at_rows(i, offset=0):
        return pl.ds(pl.multiple_of(i * STEP, STEP) + offset, STEP)

    def first_pass(i):
        here = at_rows(i)
        rho = [rho_ref[here, lanes(h)] for h in halves]
        en = [en_ref[here, lanes(h)] for h in halves]
        mat = [mat_ref[here, lanes(h)] for h in halves]
        sx = [vel_ref[0, here, lanes(h)] for h in halves]
        sy = [vel_ref[1, here, lanes(h)] for h in halves]
        both = [acoustic(rho[h], en[h], mat[h]) for h in halves]
        z, p = [b[0] for b in both], [b[1] for b in both]
        for h in halves:
            press_ref[0, h, here, :] = z[h]
            press_ref[1, h, here, :] = p[h]
        totals = column_sums(Wide(z), Wide(p), Wide(sx), Wide(sy), left)
        for s, total in enumerate(totals):
            for h in halves:
                sums_ref[s, h, at_rows(i, pad), :] = total.parts[h]
        return 0

    def first_chunk(c, _):
        for copy in copies(c):
            copy.wait()
        step = lambda j, _: first_pass(c * inner + j)
        return lax.fori_loop(0, inner, step, 0, unroll=BLOCK[0])

    for s in range(4):
        for h in halves:
            sums_ref[s, h, 0:pad, :] = jnp.full((pad, TILE), float(s == 0), jnp.float32)
            sums_ref[s, h, rows + pad :, :] = jnp.full((pad, TILE), float(s == 0), jnp.float32)
    lax.fori_loop(0, chunks, first_chunk, 0)

    def second_pass(i, _):
        for h in halves:
            under = [sums_ref[s, h, at_rows(i, pad - 1), :] for s in range(3)]
            over = [sums_ref[s, h, at_rows(i, pad), :] for s in (0, 1, 3)]
            nx, ny = nodes(under, [over[0], over[1], None, over[2]])
            node_ref[0, h, at_rows(i), :] = nx
            node_ref[1, h, at_rows(i), :] = ny
        return 0

    for copy in small:
        copy.wait()
    shifts_ref[...] = jnp.broadcast_to(shift_ref[...], (TILE, TILE)).T
    lax.fori_loop(0, rows // STEP, second_pass, 0, unroll=BLOCK[1])
    for h in halves:
        for d in range(2):
            node_ref[d, h, rows : rows + STEP, :] = jnp.zeros((STEP, TILE), jnp.float32)

    for k in range(4):
        for h in halves:
            pick = lambda row: (
                press_ref[k, h, row : row + 1, :]
                if k < 2
                else vel_ref[k - 2, row : row + 1, lanes(h)]
            )
            top, bottom = pick(rows - 1), pick(0)
            near_ref[k : k + 1, lanes(h)] = jnp.where(even_y, top, bottom)
            far_ref[k : k + 1, lanes(h)] = jnp.where(even_y, bottom, top)

    def third_pass(i, _):
        here = at_rows(i)
        wide = lambda ref, *at: Wide(ref[(*at, here, lanes(h))] for h in halves)
        rho, en = wide(rho_ref), wide(en_ref)
        sx, sy = wide(vel_ref, 0), wide(vel_ref, 1)
        z = Wide(press_ref[0, h, here, :] for h in halves)
        p = Wide(press_ref[1, h, here, :] for h in halves)
        lower = [Wide(node_ref[d, h, here, :] for h in halves) for d in range(2)]
        upper = [Wide(node_ref[d, h, at_rows(i, 1), :] for h in halves) for d in range(2)]
        shift = shifts_ref[here, :]
        cells = wide_cells(z, p, sx, sy, rho, en, lower, upper, right)
        for h, (conserved, scale, ends_left, ends_right) in enumerate(cells):
            for k, value in enumerate((*conserved[1:], scale, *next_weights(shift, ends_left, ends_right))):
                kept_ref[k, h, here, :] = value
        return 0

    def fourth_pass(i, _):
        here = at_rows(i)
        twice = Wide(2.0 * lim_ref[here, lanes(h)].astype(jnp.float32) + 2.0 for h in halves)
        kept = [Wide(kept_ref[k, h, here, :] for h in halves) for k in range(6)]
        rho = Wide(rho_ref[here, lanes(h)] for h in halves)
        for f, conserved in enumerate((rho, *kept[:3])):
            done = wide_field(conserved, kept[3], twice, kept[4:], left, right)
            spot = pl.ds(pl.multiple_of(f * rows + i * STEP, STEP), STEP)
            ends = done.parts[0], done.parts[-1]
            first_ref[spot, :] = jnp.where(even_x, ends[1], ends[0])
            second_ref[spot, :] = jnp.where(even_x, ends[0], ends[1])
        return 0

    lax.fori_loop(0, rows // STEP, third_pass, 0, unroll=BLOCK[2])
    lax.fori_loop(0, rows // STEP, fourth_pass, 0, unroll=BLOCK[3])


def rows_kernel(
    rho_ref, vel_ref, en_ref, mat_ref, lim_ref, owner_ref, sums_ref, node_ref, press_ref, shifts_ref,
    edge_ref, rim_ref, row_ref, edges_ref,
):
    rows, cols = rho_ref.shape
    halves = range(cols // TILE)
    pad = 8
    lane = lax.broadcasted_iota(jnp.int32, (STEP, TILE), 1)

    def edges(i, _):
        here = pl.ds(pl.multiple_of(i * STEP, STEP), STEP)
        edge = jnp.zeros((STEP, TILE), jnp.float32)
        ends = [
            [ref[(*at, here, lanes(h))].astype(jnp.float32) for h in (0, len(halves) - 1)]
            for ref, *at in ((rho_ref,), (vel_ref, 0), (vel_ref, 1), (en_ref,), (mat_ref,), (lim_ref,))
        ]
        for k, (start, stop) in enumerate(ends):
            turned = pltpu.roll(jnp.where(lane < TILE // 2, start, stop), (2 * k + 1) * EDGE, 1)
            edge = jnp.where(lane >= 2 * k * EDGE, turned, edge)
        edges_ref[here, :] = edge
        return 0

    lax.fori_loop(0, rows // STEP, edges, 0, unroll=EDGES)
    row_ref[0:1, :] = shifts_ref[...].T[0:1, :]
    column, count = lax.axis_index("gx"), lax.axis_size("gx")
    owner = owner_ref[...]
    for k, which in enumerate(((column + count - 1) % count, (column + 1) % count)):
        hits = jnp.where(owner == which, 1.0, 0.0)
        total = jnp.sum(jnp.sum(hits, axis=1, keepdims=True), axis=0, keepdims=True)
        row_ref[k + 1 : k + 2, :] = jnp.broadcast_to(total, (1, TILE))
    for r, row in enumerate((0, rows - 1)):
        at, to = slice(row, row + 1), slice(r, r + 1)
        joint = slice(1, 2) if r == 0 else slice(rows - 1, rows)
        for h in halves:
            kept = [
                press_ref[0, h, at, :], press_ref[1, h, at, :],
                vel_ref[0, at, lanes(h)], vel_ref[1, at, lanes(h)],
                rho_ref[at, lanes(h)], en_ref[at, lanes(h)],
                lim_ref[at, lanes(h)].astype(jnp.float32), shifts_ref[at, :],
                *(sums_ref[s, h, pad + row : pad + row + 1, :] for s in range(4)),
                *(node_ref[d, h, joint, :] for d in range(2)),
            ]
            for k, value in enumerate(kept):
                rim_ref[k, to, lanes(h)] = value

    edge_ref[...] = edges_ref[...].T[0 : 2 * RAW * EDGE, :]


def rim_kernel(near_ref, far_ref, kept_ref, edge_ref, first_ref, second_ref, corner_ref):
    cols = near_ref.shape[-1]
    halves = range(cols // TILE)
    even_x = lax.axis_index("gx") % 2 == 0
    level, levels = lax.axis_index("gy"), lax.axis_size("gy")
    even_y = level % 2 == 0
    near, far = near_ref[0:4, :], far_ref[0:4, :]
    below = jnp.where(level == 0, 0.0, jnp.where(even_y, far, near))
    above = jnp.where(level == levels - 1, 0.0, jnp.where(even_y, near, far))

    lane = lax.broadcasted_iota(jnp.int32, (8, TILE), 1)
    bottom = lax.broadcasted_iota(jnp.int32, (8, TILE), 0) == 0
    left = lambda a: Wide(wide_left(lane, a.parts))
    right = lambda a: Wide(wide_right(lane, a.parts))

    kept = [Wide(kept_ref[k, :, lanes(h)] for h in halves) for k in range(14)]
    z, p, sx, sy, rho, en, lim, shift = kept[:8]
    own, joint = kept[8:12], kept[12:14]
    outer = [
        Wide(jnp.where(bottom, cut(below[k : k + 1, :], h), cut(above[k : k + 1, :], h)) for h in halves)
        for k in range(4)
    ]
    outer = column_sums(*outer, left)
    under, over = [], []
    for a, b in zip(outer, own):
        under.append(Wide(jnp.where(bottom, x, y) for x, y in zip(a.parts, b.parts)))
        over.append(Wide(jnp.where(bottom, y, x) for x, y in zip(a.parts, b.parts)))
    fresh = [nodes([q.parts[h] for q in under], [q.parts[h] for q in over]) for h in halves]
    fresh = [Wide(q) for q in zip(*fresh)]
    lower = [Wide(jnp.where(bottom, x, y) for x, y in zip(a.parts, b.parts)) for a, b in zip(fresh, joint)]
    upper = [Wide(jnp.where(bottom, y, x) for x, y in zip(a.parts, b.parts)) for a, b in zip(fresh, joint)]
    cells = wide_cells(z, p, sx, sy, rho, en, lower, upper, right)
    weights = [next_weights(shift.parts[h], *cells[h][2:]) for h in halves]
    weights = [Wide(w) for w in zip(*weights)]
    twice = Wide(2.0 * q + 2.0 for q in lim.parts)
    scale = Wide(c[1] for c in cells)
    for f in range(4):
        conserved = Wide(c[0][f] for c in cells)
        done = wide_field(conserved, scale, twice, weights, left, right)
        ends = done.parts[0][0:2, :], done.parts[-1][0:2, :]
        first_ref[2 * f : 2 * f + 2, :] = jnp.where(even_x, ends[1], ends[0])
        second_ref[2 * f : 2 * f + 2, :] = jnp.where(even_x, ends[0], ends[1])

    halo = jnp.concatenate([below, above], axis=0)
    corner = pltpu.roll(jnp.where(lane < TILE // 2, cut(halo, 0), cut(halo, len(halves) - 1)), EDGE, 1)
    corner = jnp.concatenate([corner, jnp.zeros((TILE - 8, TILE), jnp.float32)], axis=0)
    corner_t = corner.T[0 : 2 * EDGE, :]
    corner_ref[...] = corner_t
    for k in range(RAW + 1):
        at = 2 * k * EDGE
        if k < RAW:
            right_edge, left_edge = edge_ref[at : at + EDGE, :], edge_ref[at + EDGE : at + 2 * EDGE, :]
        else:
            right_edge, left_edge = corner_t[0:EDGE, :], corner_t[EDGE:, :]
        spot = slice(8 + k * EDGE, 8 + (k + 1) * EDGE)
        first_ref[spot, :] = jnp.where(even_x, right_edge, left_edge)
        second_ref[spot, :] = jnp.where(even_x, left_edge, right_edge)


def edge_kernel(edge_ref, corner_ref, from_near_ref, from_far_ref, row_ref, patch_ref, window_ref):
    rows = patch_ref.shape[0]
    even_x = lax.axis_index("gx") % 2 == 0
    span = SPAN

    def window(k):
        spot = slice(8 + k * EDGE, 8 + (k + 1) * EDGE)
        own, at = (edge_ref, 2 * k * EDGE) if k < RAW else (corner_ref, 0)
        right_end, left_end = own[at : at + EDGE, :], own[at + EDGE : at + 2 * EDGE, :]
        near, far = from_near_ref[spot, :], from_far_ref[spot, :]
        window_ref[k, 0:EDGE, :] = jnp.where(even_x, far, near)
        window_ref[k, EDGE : 2 * EDGE, :] = left_end
        window_ref[k, 2 * EDGE : 3 * EDGE, :] = right_end
        window_ref[k, 3 * EDGE : 4 * EDGE, :] = jnp.where(even_x, near, far)
        window_ref[k, 4 * EDGE : span, :] = right_end[0 : span - 4 * EDGE, :]
        return window_ref[k, :, :]

    left = lambda a: pltpu.roll(a, 1, 0)
    right = lambda a: pltpu.roll(a, span - 1, 0)
    rho, sx, sy, en, mat, lim = (window(k) for k in range(RAW))
    halo = window(RAW)
    z, p = acoustic(rho, en, mat)
    own = column_sums(z, p, sx, sy, left)
    spread = lambda k: jnp.broadcast_to(halo[:, k : k + 1], (span, rows))
    below = column_sums(*(spread(k) for k in range(4)), left)
    above = column_sums(*(spread(k) for k in range(4, 8)), left)
    lane = lax.broadcasted_iota(jnp.int32, (span, rows), 1)
    under = [jnp.where(lane == 0, b, pltpu.roll(a, 1, 1)) for a, b in zip(own, below)]
    over = [jnp.where(lane == rows - 1, b, pltpu.roll(a, rows - 1, 1)) for a, b in zip(own, above)]
    conserved, scale, ends_left, ends_right = cell_update(
        z, p, sx, sy, rho, en, nodes(under, own), nodes(own, over), right
    )
    weights = next_weights(row_ref[0:1, :], ends_left, ends_right)
    fields = [remapped_field(q, scale, 2.0 * lim + 2.0, weights, left, right) for q in conserved]
    fields.append(jnp.zeros((TILE - 4 * span, rows), jnp.float32))
    patch_ref[...] = jnp.concatenate(fields, axis=0).T


def merge_kernel(
    first_ref, second_ref, from_near_ref, from_far_ref,
    rim_first_ref, rim_second_ref, rim_near_ref, rim_far_ref, patch_ref,
    row_ref, out_hbm, out_ref, sems,
):
    rows = out_ref.shape[1]
    span = SPAN
    chunks, inner = rows // CHUNK, CHUNK // STEP
    even_x = lax.axis_index("gx") % 2 == 0
    to_left, to_right = row_ref[1:2, :], row_ref[2:3, :]

    def put(here, row, patch, pick):
        goes_left, goes_right = row < to_left, row >= rows - to_right
        lane = lax.broadcasted_iota(jnp.int32, patch.shape, 1)
        head, tail = lane < 3, lane >= TILE - 2
        for f in range(4):
            at_left = pltpu.roll(patch, (-(span * f + EDGE)) % TILE, 1)
            at_right = pltpu.roll(patch, (-(span * f + 3 * EDGE)) % TILE, 1)
            first, second, near, far = pick(f)
            own_0 = jnp.where(head, at_left, jnp.where(even_x, second, first))
            own_1 = jnp.where(tail, at_right, jnp.where(even_x, first, second))
            before = jnp.where(tail, at_left, jnp.where(even_x, far, near))
            after = jnp.where(head, at_right, jnp.where(even_x, near, far))
            out_ref[f, here, lanes(0)] = jnp.where(
                goes_right, before, jnp.where(goes_left, own_1, own_0)
            )
            out_ref[f, here, lanes(1)] = jnp.where(
                goes_right, own_0, jnp.where(goes_left, after, own_1)
            )

    row_in = lax.broadcasted_iota(jnp.int32, (STEP, TILE), 0)

    whole = (first_ref, second_ref, from_near_ref, from_far_ref)
    rims = (rim_first_ref, rim_second_ref, rim_near_ref, rim_far_ref)

    def one(i):
        here = pl.ds(pl.multiple_of(i * STEP, STEP), STEP)

        def pick(f):
            spot = pl.ds(pl.multiple_of(f * rows + i * STEP, STEP), STEP)
            return [ref[spot, :] for ref in whole]

        put(here, (row_in + i * STEP).astype(jnp.float32), patch_ref[here, :], pick)
        return 0

    def rim(r):
        row = r * (rows - 1)
        here = slice(row, row + 1)
        pick = lambda f: [ref[2 * f + r : 2 * f + r + 1, :] for ref in rims]
        put(here, jnp.full((1, TILE), float(row)), patch_ref[here, :], pick)

    def copy(c):
        part = pl.ds(pl.multiple_of(c * CHUNK, CHUNK), CHUNK)
        return pltpu.make_async_copy(out_ref.at[:, part, :], out_hbm.at[:, 0, part, :], sems.at[c])

    def chunk(c, _):
        lax.fori_loop(0, inner, lambda j, _: one(c * inner + j), 0, unroll=MERGE)
        pl.when(c == 0)(lambda: rim(0))
        pl.when(c == chunks - 1)(lambda: rim(1))
        copy(c).start()
        return 0

    lax.fori_loop(0, chunks, chunk, 0)
    for c in range(chunks):
        copy(c).wait()


def on_device(density, velocity, energy, material, limiter, owners, dest_tile, tile_shift):
    planes, rows, cols = density.shape
    assert planes == 1 and rows == TILE and cols == 2 * TILE
    gx, gy = lax.axis_size("gx"), lax.axis_size("gy")
    f32 = jnp.float32
    vmem = pl.BlockSpec(memory_space=pltpu.VMEM)
    hbm = pl.BlockSpec(memory_space=pltpu.HBM)
    shape = lambda *dims: jax.ShapeDtypeStruct(dims, f32)
    params = pltpu.CompilerParams(vmem_limit_bytes=VMEM_LIMIT)
    chunks = rows // LOAD
    stay = lambda array: pltpu.with_memory_space_constraint(array, pltpu.HBM)

    tile = shape(4 * rows, TILE)
    i32 = lambda *dims: jax.ShapeDtypeStruct(dims, jnp.int32)
    tile = shape(4 * rows, TILE)
    first, second, near, far, *inner = pl.pallas_call(
        block_kernel,
        in_specs=[hbm] * 7,
        out_specs=[vmem] * 14,
        out_shape=[
            tile,
            tile,
            shape(8, cols),
            shape(8, cols),
            shape(rows, cols),
            shape(2, rows, cols),
            shape(rows, cols),
            i32(rows, cols),
            i32(rows, cols),
            i32(rows * cols // TILE // TILE, TILE),
            shape(4, 2, rows + 16, TILE),
            shape(2, 2, rows + 8, TILE),
            shape(2, 2, rows, TILE),
            shape(rows, TILE),
        ],
        scratch_shapes=[
            pltpu.VMEM((1, rows), f32),
            pltpu.VMEM((6, 2, rows, TILE), f32),
            pltpu.SemaphoreType.DMA((5, chunks)),
            pltpu.SemaphoreType.DMA((2,)),
        ],
        compiler_params=params,
        name="block",
    )(*map(stay, (density, velocity, energy, material, limiter, tile_shift, owners.reshape(-1, TILE))))
    from_near = lax.ppermute(first, "gx", near_pairs(gx))
    from_far = lax.ppermute(second, "gx", far_pairs(gx))
    edge, kept, per_row = pl.pallas_call(
        rows_kernel,
        in_specs=[vmem] * 10,
        out_specs=[vmem] * 3,
        out_shape=[
            shape(2 * RAW * EDGE, TILE),
            shape(14, 8, cols),
            shape(8, TILE),
        ],
        scratch_shapes=[pltpu.VMEM((rows, TILE), f32)],
        compiler_params=params,
        name="outer",
    )(*inner)
    near = lax.ppermute(near, "gy", near_pairs(gy))
    far = lax.ppermute(far, "gy", far_pairs(gy))

    small = shape(8 + (RAW + 1) * EDGE, TILE)
    small_first, small_second, corner = pl.pallas_call(
        rim_kernel,
        in_specs=[vmem] * 4,
        out_specs=[vmem] * 3,
        out_shape=[small, small, shape(2 * EDGE, TILE)],
        compiler_params=params,
        name="rim",
    )(near, far, kept, edge)
    small_near = lax.ppermute(small_first, "gx", near_pairs(gx))
    small_far = lax.ppermute(small_second, "gx", far_pairs(gx))

    patch = pl.pallas_call(
        edge_kernel,
        in_specs=[vmem] * 5,
        out_specs=vmem,
        out_shape=shape(rows, TILE),
        scratch_shapes=[pltpu.VMEM((RAW + 1, SPAN, rows), f32)],
        compiler_params=params,
        name="edge",
    )(edge, corner, small_near, small_far, per_row)

    return pl.pallas_call(
        merge_kernel,
        in_specs=[vmem] * 10,
        out_specs=hbm,
        out_shape=shape(4, planes, rows, cols),
        scratch_shapes=[pltpu.VMEM((4, rows, cols), f32), pltpu.SemaphoreType.DMA((rows // CHUNK,))],
        compiler_params=params,
        name="merge",
    )(
        first, second, from_near, from_far,
        small_first, small_second, small_near, small_far, patch, per_row,
    )


def solution(mesh):
    assert mesh.shape["gx"] % 2 == 0 and mesh.shape["gy"] % 2 == 0
    placed = (
        P(None, "gy", "gx"),
        P(None, None, "gy", "gx"),
        P(None, "gy", "gx"),
        P(None, "gy", "gx"),
        P(None, "gy", "gx"),
        P(("gx", "gy")),
        P(("gx", "gy")),
        P(None, "gy"),
    )
    return jax.shard_map(
        on_device, mesh=mesh, in_specs=placed, out_specs=P(None, None, "gy", "gx"), check_vma=False
    )
```
